32 devices in a mesh: batch: 4 (over y, core), seq: 8 (over z, x).
Axes of the slice: x: 2, y: 2, z: 4, core: 2. Of those that a mesh axis runs over, the one named last changes fastest.
Arguments:
- tokens: bfloat16 [4, 1024, 1024], P('batch', 'seq'), may hold values from -6 to 6
- w_query: bfloat16 [512, 512], replicated, may hold values from -0.25 to 0.25
- w_value: bfloat16 [512, 512], replicated, may hold values from -0.25 to 0.25
- w_out: bfloat16 [512, 512], replicated, may hold values from -0.25 to 0.25
- long_filter: float32 [512, 1024], P('seq'), may hold values from -0.1875 to 0.1875
- cotangent: bfloat16 [4, 1024, 1024], P('batch', 'seq'), may hold values from -6 to 6
Outputs:
- block_out: bfloat16 [4, 1024, 1024], P('batch', 'seq')
- grad_tokens: bfloat16 [4, 1024, 1024], P('batch', 'seq')
- grad_query: float32 [512, 512], P('seq')
- grad_value: float32 [512, 512], P('seq')
- grad_out: float32 [512, 512], P('seq')
- grad_filter: float32 [512, 1024], P('seq')
The draws below stay inside these ranges and needn't reach their ends.
All inputs are finite; a program needn't handle non-finite values.
Results may differ from the reference program's by a relative error of at most 0.017.
Values may be sent and summed in bfloat16 or wider, within the bound.
A program may use at most 64 MiB of HBM per device.

```python
import jax
import jax.numpy as jnp

D = 1024
HALF = 512
LENGTH = 1024
SEQS = 4


def raised(entries, stream_key, source, target, shards_of, factor):
    owner, partner = [(jnp.arange(entries.shape[dim]) // (entries.shape[dim] // shards_of)).reshape([-1 if axis == dim else 1 for axis in range(entries.ndim)]) for dim in (source, target)]
    chosen = jax.random.permutation(stream_key, shards_of)[partner]
    strong = (owner == chosen) | (owner == (partner + shards_of // 2) % shards_of)
    return jnp.where(strong, factor * entries, entries)


def block_scale(own_key, dims, shards, smallest, top_value):
    gain = 1.0
    for position, shards_of in shards:
        draws = jax.random.uniform(jax.random.fold_in(jax.random.fold_in(own_key, 6), position), (shards_of,), jnp.float32, smallest / len(shards), top_value / len(shards))
        gain = gain * jnp.repeat(jnp.exp(draws), dims[position] // shards_of).reshape((-1,) + (1,) * (len(dims) - 1 - position))
    return gain


def gaussian(own_key, dims, scale, most, pieces=(), kind=jnp.bfloat16):
    level = block_scale(own_key, dims, pieces, -0.22, 0.18) if pieces else 1.0
    drawn = jax.random.normal(own_key, dims, jnp.float32) * scale * level
    return jnp.minimum(jnp.maximum(drawn, -most), most).astype(kind)


def noise_with(key, dims, deviation, limit, split, heavy, held_as=jnp.bfloat16):
    entries = deviation * jax.random.normal(key, dims, jnp.float32)
    if split:
        entries = entries * block_scale(key, dims, split, -0.22, 0.18)
    return jnp.clip(raised(entries, jax.random.fold_in(key, 3), *heavy), -limit, limit).astype(held_as)


def setup_inputs(seed: int = 0) -> dict:
    arg_keys = jax.random.split(jax.random.key(seed), 7)
    return {
        "tokens": noise_with(arg_keys[0], (SEQS, LENGTH, D), 1.0, 6.0, ((0, 4), (1, 8)), (1, 2, 8, 2.0)),
        "w_query": gaussian(arg_keys[1], (HALF, HALF), HALF ** -0.5, 0.25),
        "w_value": gaussian(arg_keys[2], (HALF, HALF), HALF ** -0.5, 0.25),
        "w_out": gaussian(arg_keys[3], (HALF, HALF), HALF ** -0.5, 0.25),
        "long_filter": gaussian(arg_keys[4], (HALF, LENGTH), LENGTH ** -0.5, 0.1875, ((0, 8),), jnp.float32),
        "cotangent": gaussian(arg_keys[5], (SEQS, LENGTH, D), 1.0, 6.0, ((0, 4), (1, 8))),
    }


def rc_flip(block):
    return block[::-1, ::-1]


def reference(tokens, w_query, w_value, w_out, long_filter, cotangent):
    floats = jnp.float32
    halves = jnp.bfloat16
    half = HALF
    length = LENGTH
    period = 2 * LENGTH
    scale = (2.0 * SEQS * LENGTH) ** -0.5
    taps = jnp.fft.fft(long_filter, n=period, axis=1)
    query_weight = w_query.astype(floats)
    value_weight = w_value.astype(floats)
    out_weight = w_out.astype(floats)
    total_query = jnp.zeros((half, half), floats)
    total_value = jnp.zeros((half, half), floats)
    total_out = jnp.zeros((half, half), floats)
    total_filter = jnp.zeros((half, length), floats)
    outputs = []
    gradients = []
    for sequence in range(SEQS):
        source = tokens[sequence]
        front = source[:, :half]
        back = source[:, half:]
        strands = jnp.stack([front, rc_flip(back)]).astype(floats)
        query = jnp.einsum('stk,kh->sht', strands, query_weight).astype(halves)
        value = jnp.einsum('stk,kh->sht', strands, value_weight).astype(halves)
        value_spec = jnp.fft.fft(value.astype(floats), n=period, axis=2)
        conv = jnp.fft.ifft(value_spec * taps[None], axis=2)[:, :, :length].real.astype(halves)
        gated = (query.astype(floats) * conv.astype(floats)).astype(halves)
        projected = jnp.einsum('sht,hk->stk', gated.astype(floats), out_weight)
        block = jnp.concatenate([front.astype(floats) + projected[0], back.astype(floats) + rc_flip(projected[1])], axis=1)
        outputs.append(block.astype(halves))
        upstream = cotangent[sequence]
        grad_strands = jnp.stack([upstream[:, :half], rc_flip(upstream[:, half:])]).astype(floats)
        grad_gated = jnp.einsum('stk,hk->sht', grad_strands, out_weight).astype(halves)
        grad_query_t = (grad_gated.astype(floats) * conv.astype(floats)).astype(halves)
        grad_conv = (grad_gated.astype(floats) * query.astype(floats)).astype(halves)
        grad_spec = jnp.fft.fft(grad_conv.astype(floats), n=period, axis=2)
        grad_value_t = jnp.fft.ifft(grad_spec * jnp.conj(taps)[None], axis=2)[:, :, :length].real.astype(halves)
        filter_spec = jnp.sum(jnp.conj(value_spec) * grad_spec, axis=0)
        total_filter = total_filter + jnp.fft.ifft(filter_spec, axis=1)[:, :length].real.astype(floats)
        input_grad = jnp.einsum('sht,kh->stk', grad_query_t.astype(floats), query_weight) + jnp.einsum('sht,kh->stk', grad_value_t.astype(floats), value_weight)
        grad_block = jnp.concatenate([upstream[:, :half].astype(floats) + input_grad[0], upstream[:, half:].astype(floats) + rc_flip(input_grad[1])], axis=1)
        gradients.append(grad_block.astype(halves))
        total_query = total_query + jnp.einsum('stk,sht->kh', strands, grad_query_t.astype(floats))
        total_value = total_value + jnp.einsum('stk,sht->kh', strands, grad_value_t.astype(floats))
        total_out = total_out + jnp.einsum('sht,stk->hk', gated.astype(floats), grad_strands)
    return (jnp.stack(outputs), jnp.stack(gradients), total_query * scale, total_value * scale, total_out * scale, total_filter * scale)
```

```python
import functools
import math

import jax
import jax.numpy as jnp
import numpy as np
from jax import lax
from jax.experimental import pallas as pl
from jax.experimental.pallas import tpu as pltpu
from jax.sharding import PartitionSpec as P

precise = lax.Precision.HIGH


def swapped(x, axis, stride):
    return lax.ppermute(x, axis, [(i, i ^ 1 << stride) for i in range(lax.axis_size(axis))])


def angle_tables(count_rows, count_cols, period):
    left = lax.broadcasted_iota(jnp.int32, (count_rows, count_cols), 0)
    right = lax.broadcasted_iota(jnp.int32, (count_rows, count_cols), 1)
    turns = left * right % period
    angle = turns.astype(jnp.float32) * (2.0 * math.pi / period)
    return (jnp.cos(angle), jnp.sin(angle))


def rotation(cosines, sines, direction):
    upper = jnp.stack([cosines, direction * sines])
    lower_row = jnp.stack([-direction * sines, cosines])
    return jnp.stack([upper, lower_row])


def split_sizes(length):
    period = 2 * length
    first = 1 << (period.bit_length() - 1 + 1) // 2
    return (first, period // first)


def make_tables(first, second):
    cos_first, sin_first = angle_tables(first, first, first)
    cos_twist, sin_twist = angle_tables(first, second, first * second)
    cos_second, sin_second = angle_tables(second, second, second)
    forward_first = rotation(cos_first, sin_first, 1.0)
    inverse_first = rotation(cos_first, sin_first, -1.0)
    forward_second = rotation(cos_second, sin_second, 1.0)
    inverse_second = rotation(cos_second, sin_second, -1.0)
    return (forward_first, inverse_first, forward_second, inverse_second, cos_twist, sin_twist)


def forward_spectrum(signal, tables, first, second):
    forward_first, inverse_first, forward_second, inverse_second, cos_twist, sin_twist = tables
    lower = first // 2
    folded = signal.reshape(2, signal.shape[1], lower, second)
    section = jnp.einsum("brnm,abnk->arkm", folded, forward_first[:, :, :lower], precision=precise)
    turned = jnp.stack(
        [
            section[0] * cos_twist + section[1] * sin_twist,
            section[1] * cos_twist - section[0] * sin_twist,
        ]
    )
    return jnp.einsum("brkm,abmj->arkj", turned, forward_second, precision=precise)


def inverse_spectrum(spectrum, tables, first, second, both):
    forward_first, inverse_first, forward_second, inverse_second, cos_twist, sin_twist = tables
    lower = first // 2
    rows = spectrum.shape[1]
    inner = jnp.einsum("brkj,abjm->arkm", spectrum, inverse_second, precision=precise)
    turned = jnp.stack(
        [inner[0] * cos_twist - inner[1] * sin_twist, inner[1] * cos_twist + inner[0] * sin_twist]
    )
    if both:
        signal = jnp.einsum(
            "brkm,abkn->arnm", turned, inverse_first[:, :, :, :lower], precision=precise
        )
        return (signal / (first * second)).reshape(2, rows, lower * second)
    signal = jnp.einsum("brkm,bkn->rnm", turned, inverse_first[0][:, :, :lower], precision=precise)
    return (signal / (first * second)).reshape(rows, lower * second)


def complex_product(left, right):
    return jnp.stack(
        [left[0] * right[0] - left[1] * right[1], left[0] * right[1] + left[1] * right[0]]
    )


def conjugate_product(left, right):
    return jnp.stack(
        [left[0] * right[0] + left[1] * right[1], left[0] * right[1] - left[1] * right[0]]
    )


def mirror(array, seq_dim):
    moved = array
    for bit_index in range(lax.axis_size("seq").bit_length() - 1):
        moved = swapped(moved, "seq", bit_index)
    return jnp.flip(moved, axis=seq_dim)


def to_channels(stacked):
    return lax.all_to_all(stacked, "seq", split_axis=1, concat_axis=2, tiled=True)


def to_tokens(stacked):
    return lax.all_to_all(stacked, "seq", split_axis=2, concat_axis=1, tiled=True)


def body(tokens, w_query, w_value, w_out, long_filter, cotangent):
    floats = jnp.float32
    halves = jnp.bfloat16
    half = w_query.shape[0]
    seq_count = lax.axis_size("seq")
    batch_count = lax.axis_size("batch")
    length = tokens.shape[1] * seq_count
    first, second = split_sizes(length)
    tables = make_tables(first, second)
    scale = (2.0 * batch_count * length) ** (-0.5)
    source = tokens[0]
    front = source[:, :half]
    back = source[:, half:]
    back_strand = mirror(back, 0)[:, ::-1]
    strands = jnp.stack([front, back_strand])
    query = jnp.einsum("stk,kh->sht", strands, w_query, preferred_element_type=floats).astype(
        halves
    )
    value = jnp.einsum("stk,kh->sht", strands, w_value, preferred_element_type=floats).astype(
        halves
    )
    value_sig = to_channels(value).astype(floats)
    value_spec = forward_spectrum(value_sig, tables, first, second)
    taps_spec = forward_spectrum(
        jnp.stack([long_filter, jnp.zeros_like(long_filter)]), tables, first, second
    )
    conv_sig = inverse_spectrum(complex_product(value_spec, taps_spec), tables, first, second, True)
    conv_tok = to_tokens(conv_sig.astype(halves))
    gated = (query.astype(floats) * conv_tok.astype(floats)).astype(halves)
    gated_back = mirror(gated[1], 1)
    out_front = jnp.einsum("ht,hk->tk", gated[0], w_out, preferred_element_type=floats)
    out_back = jnp.einsum("ht,hk->tk", gated_back, w_out, preferred_element_type=floats)
    block_out = jnp.concatenate(
        [front.astype(floats) + out_front, back.astype(floats) + out_back[:, ::-1]], axis=1
    ).astype(halves)[None]
    upstream = cotangent[0]
    up_front = upstream[:, :half]
    up_back = upstream[:, half:]
    grad_back = mirror(up_back, 0)[:, ::-1]
    grad_strands = jnp.stack([up_front, grad_back])
    grad_gated = jnp.einsum(
        "stk,hk->sht", grad_strands, w_out, preferred_element_type=floats
    ).astype(halves)
    grad_query_t = (grad_gated.astype(floats) * conv_tok.astype(floats)).astype(halves)
    grad_conv = (grad_gated.astype(floats) * query.astype(floats)).astype(halves)
    grad_sig = to_channels(grad_conv).astype(floats)
    grad_spec = forward_spectrum(grad_sig, tables, first, second)
    value_grad_sig = inverse_spectrum(
        conjugate_product(taps_spec, grad_spec), tables, first, second, True
    )
    filter_part = (
        inverse_spectrum(conjugate_product(value_spec, grad_spec), tables, first, second, False)
        * scale
    )
    grad_value_t = to_tokens(value_grad_sig.astype(halves))
    front_in = jnp.einsum(
        "ht,kh->tk", grad_query_t[0], w_query, preferred_element_type=floats
    ) + jnp.einsum("ht,kh->tk", grad_value_t[0], w_value, preferred_element_type=floats)
    paired = jnp.stack([grad_query_t[1], grad_value_t[1]])
    paired = mirror(paired, 2)
    back_in = jnp.einsum(
        "ht,kh->tk", paired[0], w_query, preferred_element_type=floats
    ) + jnp.einsum("ht,kh->tk", paired[1], w_value, preferred_element_type=floats)
    grad_tokens = jnp.concatenate(
        [up_front.astype(floats) + front_in, up_back.astype(floats) + back_in[:, ::-1]], axis=1
    ).astype(halves)[None]
    term_query = jnp.einsum("stk,sht->kh", strands, grad_query_t, preferred_element_type=floats)
    term_value = jnp.einsum("stk,sht->kh", strands, grad_value_t, preferred_element_type=floats)
    term_out = jnp.einsum("sht,stk->hk", gated, grad_strands, preferred_element_type=floats)
    share = lax.psum_scatter(
        jnp.concatenate([term_query, term_value, term_out], axis=1) * scale,
        "seq",
        scatter_dimension=0,
        tiled=True,
    )
    share, filter_total = (
        lax.psum(share.astype(jnp.bfloat16), "batch").astype(jnp.float32),
        lax.psum(filter_part.astype(jnp.bfloat16), "batch").astype(jnp.float32),
    )
    return (
        block_out,
        grad_tokens,
        share[:, :half],
        share[:, half : 2 * half],
        share[:, 2 * half :],
        filter_total,
    )

MESH = pl.DeviceIdType.MESH


def angle_parts(length):
    step = 1 << (length.bit_length() - 1) // 2
    angle = np.pi * (np.arange(length) + 0.5)[None] / length
    coarse = np.arange(length // step)[:, None] * step * angle
    fine = np.arange(step)[:, None] * angle
    return (
        np.stack([np.cos(coarse), np.sin(coarse)]).astype(np.float32),
        np.stack([np.cos(fine), np.sin(fine)]).astype(np.float32),
    )


def matmul(left, right):
    return jnp.dot(left, right, preferred_element_type=jnp.float32)


def matmul_t(left, right):
    return lax.dot_general(
        left, right, (((1,), (1,)), ((), ())), preferred_element_type=jnp.float32
    )


def times(x, h, conj):
    size = x.shape[1] // 2
    xr, xs, hr, hs = x[:, :size], x[:, size:], h[:, :size], h[:, size:]
    if conj:
        return xr * hr + xs * hs, xs * hr - xr * hs
    return xr * hr - xs * hs, xr * hs + xs * hr


def fused(
    scale,
    tok_in, wq_in, wv_in, wo_in, taps_in, cot_in, coarse_in, fine_in,
    block_out, grad_out, out_w, out_f,
    block, grad_tok, osem,
    tok, wq, wv, wo, taps, cot, coarse, fine, lsem,
    table, strands, ups, strands_t, query, gates, send1, recv1, send2, recv2,
    both_taps, vspec, gspec, hspec, yspec, fspec,
    ssem1, rsem1, lsem1, ssem2, rsem2, lsem2, ssem_t, rsem_t,
    acc, kept, send_a, recv_a, send_b, recv_b, send_c, recv_c, full,
    acc_f, kept_f, last_f, send_af, recv_af, send_bf, recv_bf, send_cf, recv_cf, full_f,
    ssem_a, rsem_a, ssem_b, rsem_b, ssem_c, rsem_c, ssem_d, rsem_d,
):
    peers, batches = lax.axis_size("seq"), lax.axis_size("batch")
    me, seat = lax.axis_index("seq"), lax.axis_index("batch")
    here, half = tok.shape[0], wq.shape[0]
    f32, b16 = jnp.float32, jnp.bfloat16
    own = half // peers
    length = here * peers
    quarter = own // batches
    mates = peers // 2
    wide = mates * here
    rows = 2 * own
    side, seat_in_side = me // mates, lax.rem(me, mates)
    other = 1 - side
    sign = (2 * side - 1).astype(f32)
    column, level = lax.rem(me, 2), me // 2
    levels = peers // 2
    low, high = lax.rem(seat, 2), seat // 2
    slot = 2 * low + high

    barrier = pltpu.get_barrier_semaphore()
    across = me + 1 - 2 * column
    facing = seat + 2 - 4 * high
    for r in range(1, peers):
        pl.semaphore_signal(
            barrier, inc=1, device_id={"seq": lax.rem(me + r, peers)}, device_id_type=MESH
        )
    for r in range(1, batches):
        pl.semaphore_signal(
            barrier, inc=1, device_id={"batch": lax.rem(seat + r, batches)}, device_id_type=MESH
        )
    pl.semaphore_signal(
        barrier, inc=1, device_id={"seq": across, "batch": facing}, device_id_type=MESH
    )
    loads = {}
    pairs = (
        ("tok", tok_in, tok), ("wv", wv_in, wv), ("taps", taps_in, taps), ("cot", cot_in, cot),
        ("wo", wo_in, wo), ("wq", wq_in, wq), ("coarse", coarse_in, coarse), ("fine", fine_in, fine),
    )
    for index, (name, src, dst) in enumerate(pairs):
        loads[name] = pltpu.make_async_copy(src, dst, lsem.at[index])
        loads[name].start()

    def remote(src, dst, ssem, rsem, **device):
        copy = pltpu.make_async_remote_copy(
            src_ref=src, dst_ref=dst, send_sem=ssem, recv_sem=rsem,
            device_id=device, device_id_type=MESH,
        )
        copy.start()
        return copy

    def local(src, dst, sem):
        copy = pltpu.make_async_copy(src, dst, sem)
        copy.start()
        return copy

    def wait(copies):
        for c in copies:
            c.wait()

    flip = (
        lax.broadcasted_iota(jnp.int32, (half, half), 0)
        + lax.broadcasted_iota(jnp.int32, (half, half), 1)
        == half - 1
    ).astype(f32).astype(b16)

    def stage_rows(index, x):
        turned = x.T
        for bh in range(2):
            for bj in range(mates):
                start = (bh * mates + bj) * own
                send1[index, bj, bh] = turned[start : start + own]

    loads["tok"].wait()
    strands[:here] = tok[:, :half]
    strands[here:] = matmul(tok[:, half:], flip).astype(b16)
    loads["wv"].wait()
    value = matmul(strands[...], wv[...]).astype(b16)
    stage_rows(0, value[:here])
    stage_rows(1, value[here:])
    loads["taps"].wait()
    both_taps[pl.ds(side, 1)] = taps[...].astype(b16).reshape(1, batches, quarter, length)
    pl.semaphore_wait(barrier, peers + batches - 1)

    partner = lax.rem(me + mates, peers)
    tap_copy = remote(
        both_taps.at[side, seat], both_taps.at[side, seat], ssem_t.at[0], rsem_t.at[0], seq=partner
    )

    def out1_cross(d):
        c = 2 * d + (side if d == 0 else other)
        copies = []
        for r in range(mates):
            q = lax.rem(seat_in_side + r, mates)
            copies.append(
                remote(
                    send1.at[c, q], recv1.at[c, me], ssem1.at[d, mates + r], rsem1.at[d, mates + r],
                    seq=other * mates + q,
                )
            )
        return copies

    def out1_own(d):
        pair = pl.ds(2 * d, 2)
        copies = []
        for r in range(1, mates):
            q = lax.rem(seat_in_side + r, mates)
            copies.append(
                remote(
                    send1.at[pair, q], recv1.at[pair, me], ssem1.at[d, r], rsem1.at[d, r],
                    seq=side * mates + q,
                )
            )
        copies.append(local(send1.at[pair, seat_in_side], recv1.at[pair, me], lsem1.at[d]))
        return copies

    def out2(k, c):
        copies = []
        for r in range(1, mates):
            q = lax.rem(seat_in_side + r, mates)
            copies.append(
                remote(
                    send2.at[c, q], recv2.at[c, seat_in_side], ssem2.at[k, r], rsem2.at[k, r],
                    seq=side * mates + q,
                )
            )
        copies.append(local(send2.at[c, seat_in_side], recv2.at[c, seat_in_side], lsem2.at[k]))
        return copies

    own_v = out1_own(0)
    cross_v = out1_cross(0)

    for name in ("cot", "wo", "wq"):
        loads[name].wait()
    ups[:here] = cot[:, :half]
    ups[here:] = matmul(cot[:, half:], flip).astype(b16)
    query[...] = matmul(strands[...], wq[...]).astype(b16)
    gates[...] = matmul_t(ups[...], wo[...]).astype(b16)
    grad_conv = (gates[...].astype(f32) * query[...].astype(f32)).astype(b16)
    stage_rows(2, grad_conv[:here])
    stage_rows(3, grad_conv[here:])
    own_g = out1_own(1)
    cross_g = out1_cross(1)

    for name in ("coarse", "fine"):
        loads[name].wait()
    count, step = coarse.shape[1], fine.shape[1]

    @pl.loop(0, count)
    def _(a):
        ca, sa = coarse[0, pl.ds(a, 1), :], coarse[1, pl.ds(a, 1), :]
        at = pl.ds(pl.multiple_of(a * step, step), step)
        table[at, :length] = (ca * fine[0] - sa * fine[1]).astype(b16)
        table[at, length:] = (sa * fine[0] + ca * fine[1]).astype(b16)

    tap_copy.wait()
    tap_copies = [
        remote(
            both_taps.at[other, seat], both_taps.at[other, seat], ssem_t.at[r], rsem_t.at[r],
            batch=lax.rem(seat + r, batches),
        )
        for r in range(1, batches)
    ]
    strands_t[...] = strands[...].T

    def rows_at(i):
        return pl.ds(pl.multiple_of(i * rows, rows), rows)

    def table_of(which):
        return table[pl.ds(pl.multiple_of(which * wide, wide), wide), :]

    def signal(c, which):
        return jnp.concatenate(
            [recv1[c, which * mates + i].reshape(rows, here) for i in range(mates)], axis=1
        )

    def own_signals(d):
        return jnp.concatenate([signal(2 * d, side), signal(2 * d + 1, side)], axis=0)

    def returned(k, c, spec, conj):
        r, s = times(spec, hspec[...], conj)
        yspec[k, :, :length] = r.astype(b16)
        yspec[k, :, length:] = s.astype(b16)
        back = (matmul_t(yspec[k], table_of(side)) * (1.0 / length)).astype(b16)
        for q in range(mates):
            send2[pl.ds(c, 1), q] = back[:, q * here : (q + 1) * here].reshape(1, 2, own, here)
        return out2(k, c)

    wait(own_v)
    vspec[...] = matmul(own_signals(0), table_of(side))
    wait(tap_copies)
    hspec[...] = matmul(both_taps[...].reshape(rows, length), table[...])
    hspec[:, length:] = hspec[:, length:] * sign
    self_v = returned(0, side, vspec[rows_at(side), :], True)
    wait(cross_v)
    vspec[rows_at(other), :] = vspec[rows_at(other), :] + matmul(
        signal(other, other), table_of(other)
    )
    full_v = returned(1, other, vspec[rows_at(other), :], False)

    wait(own_g)
    gspec[...] = matmul(own_signals(1), table_of(side))
    self_g = returned(2, 2 + other, gspec[rows_at(other), :], True)
    r0, s0 = times(gspec[rows_at(other), :], vspec[rows_at(other), :], True)
    r1, s1 = times(gspec[rows_at(side), :], vspec[rows_at(side), :], True)
    fspec[:, :length] = (r0 + r1).astype(b16)
    fspec[:, length:] = ((s0 - s1) * sign).astype(b16)
    wait(cross_g)
    gspec[rows_at(side), :] = gspec[rows_at(side), :] + matmul(
        signal(2 + side, other), table_of(other)
    )
    full_g = returned(3, 2 + side, gspec[rows_at(side), :], False)

    def part_of(bit, size):
        return pl.ds(pl.multiple_of(bit * size, size), size)

    def weight(m, product):
        acc[m] = (product * scale).reshape(levels, 2, own, half)

    def stage_a(m):
        send_a[m] = acc[m, :, :, part_of(1 - low, 2 * quarter), :].astype(b16)
        return remote(
            send_a.at[m], recv_a.at[m], ssem_a.at[m], rsem_a.at[m], batch=2 * high + 1 - low
        )

    def stage_b(m, copy):
        copy.wait()

        def pick(x, y):
            at = pl.ds(pl.multiple_of((2 * low + y) * quarter, quarter), quarter)
            mine = acc[m, :, pl.ds(x, 1), at, :]
            theirs = recv_a[m, :, pl.ds(x, 1), part_of(y, quarter), :].astype(f32)
            return (mine + theirs).reshape(levels, quarter, half)

        copies = []
        for index, (dx, dy) in enumerate(((1, 1), (1, 0), (0, 1))):
            x = 1 - column if dx else column
            y = 1 - high if dy else high
            send_b[m, index] = pick(x, y).astype(b16)
            copies.append(
                remote(
                    send_b.at[m, index], recv_b.at[m, index], ssem_b.at[m, index],
                    rsem_b.at[m, index], seq=across if dx else me, batch=facing if dy else seat,
                )
            )
        kept[m] = pick(column, high)
        return copies

    def stage_c(m, copies):
        wait(copies)
        send_c[m] = (kept[m] + jnp.sum(recv_b[m].astype(f32), axis=0)).astype(b16)
        copies = []
        for r in range(1, levels):
            z = lax.rem(level + r, levels)
            copies.append(
                remote(
                    send_c.at[m, z], recv_c.at[m, level], ssem_c.at[m, r], rsem_c.at[m, r],
                    seq=2 * z + column,
                )
            )
        recv_c[m, level] = send_c[m, level]
        return copies

    def share(m, whole):
        return [
            remote(
                whole.at[slot], whole.at[slot], ssem_d.at[m, r], rsem_d.at[m, r],
                batch=lax.rem(seat + r, batches),
            )
            for r in range(1, batches)
        ]

    def stage_d(m, copies):
        wait(copies)
        full[m, slot] = jnp.sum(recv_c[m].astype(f32), axis=0).astype(b16)
        return share(m, full.at[m])

    def leave(index, src, dst):
        return local(src, dst, osem.at[index])

    def finish(m, copies):
        wait(copies)
        return leave(m, full_f if m == 3 else full.at[m], out_f if m == 3 else out_w.at[m])

    wait(self_v)
    wait(full_v)

    def rejoin(c):
        return jnp.concatenate(
            [recv2[c, bj, bh] for bh in range(2) for bj in range(mates)], axis=0
        ).T

    conv = jnp.concatenate([rejoin(0), rejoin(1)], axis=0).astype(f32)
    grad_query = (gates[...].astype(f32) * conv).astype(b16)
    weight(0, matmul(strands_t[...], grad_query))
    a0 = stage_a(0)
    gated = (query[...].astype(f32) * conv).astype(b16)
    weight(1, matmul(gated.T, ups[...]))
    a1 = stage_a(1)
    b0 = stage_b(0, a0)
    b1 = stage_b(1, a1)
    acc_f[...] = (matmul_t(fspec[...], table[...]) * (scale / length)).reshape(2, own, length)
    send_af[...] = acc_f[:, part_of(1 - low, 2 * quarter), :].astype(b16)
    af = remote(send_af, recv_af, ssem_a.at[3], rsem_a.at[3], batch=2 * high + 1 - low)
    wait(self_g)
    wait(full_g)
    value_0, value_1 = rejoin(2), rejoin(3)
    grad_value = jnp.concatenate([value_0, value_1], axis=0)
    weight(2, matmul(strands_t[...], grad_value))
    a2 = stage_a(2)
    c0 = stage_c(0, b0)
    c1 = stage_c(1, b1)
    af.wait()
    kept_f[...] = acc_f[:, part_of(low, 2 * quarter), :] + recv_af[...].astype(f32)
    send_bf[...] = kept_f[:, part_of(1 - high, quarter), :].astype(b16)
    bf = remote(send_bf, recv_bf, ssem_b.at[3, 0], rsem_b.at[3, 0], batch=facing)
    b2 = stage_b(2, a2)
    total = strands[...].astype(f32) + matmul(gated, wo[...])
    block[:, :half] = total[:here].astype(b16)
    block[:, half:] = matmul(total[here:].astype(b16), flip).astype(b16)
    o4 = leave(4, block, block_out)
    bf.wait()
    last_f[...] = kept_f[:, part_of(high, quarter), :] + recv_bf[...].astype(f32)
    send_cf[...] = last_f[other].astype(b16)
    cf = remote(send_cf, recv_cf, ssem_c.at[3, 0], rsem_c.at[3, 0], seq=partner)
    c2 = stage_c(2, b2)
    d0 = stage_d(0, c0)
    d1 = stage_d(1, c1)
    total = ups[...].astype(f32) + matmul_t(grad_query, wq[...]) + matmul_t(grad_value, wv[...])
    grad_tok[:, :half] = total[:here].astype(b16)
    grad_tok[:, half:] = matmul(total[here:].astype(b16), flip).astype(b16)
    o5 = leave(5, grad_tok, grad_out)
    cf.wait()
    full_f[slot] = (last_f[side] + recv_cf[...].astype(f32)).astype(b16)
    df = share(3, full_f)
    d2 = stage_d(2, c2)
    o0 = finish(0, d0)
    o1 = finish(1, d1)
    o3 = finish(3, df)
    o2 = finish(2, d2)
    wait((o0, o1, o2, o3, o4, o5))


def emit(block, grad_tok, weights, filters, block_out, grad_out, out_q, out_v, out_o, out_f):
    block_out[...] = block[...]
    grad_out[...] = grad_tok[...]
    out_q[...] = weights[0].reshape(out_q.shape).astype(out_q.dtype)
    out_o[...] = weights[1].reshape(out_o.shape).astype(out_o.dtype)
    out_v[...] = weights[2].reshape(out_v.shape).astype(out_v.dtype)
    out_f[...] = filters[...].reshape(out_f.shape).astype(out_f.dtype)


def short_body(tokens, w_query, w_value, w_out, long_filter, cotangent):
    f32, b16 = jnp.float32, jnp.bfloat16
    half = w_query.shape[0]
    peers = lax.axis_size("seq")
    here = tokens.shape[1]
    length = here * peers
    own = half // peers
    scale = (2.0 * lax.axis_size("batch") * length) ** (-0.5)
    coarse, fine = angle_parts(length)
    dma = pltpu.SemaphoreType.DMA
    batches = lax.axis_size("batch")
    quarter = own // batches
    mates = levels = peers // 2
    vmem = pltpu.VMEM
    arguments = (tokens[0], w_query, w_value, w_out, long_filter, cotangent[0], coarse, fine)
    block, grad_tok, weights, filters = pl.pallas_call(
        functools.partial(fused, scale),
        out_shape=(
            jax.ShapeDtypeStruct((here, 2 * half), b16),
            jax.ShapeDtypeStruct((here, 2 * half), b16),
            jax.ShapeDtypeStruct((3, batches, quarter, half), b16),
            jax.ShapeDtypeStruct((batches, quarter, length), b16),
        ),
        in_specs=[pl.BlockSpec(memory_space=pltpu.HBM)] * 8,
        out_specs=(pl.BlockSpec(memory_space=pltpu.HBM),) * 4,
        scratch_shapes=[
            vmem((here, 2 * half), b16),
            vmem((here, 2 * half), b16),
            dma((6,)),
            *(vmem(a.shape, a.dtype) for a in arguments),
            dma((8,)),
            vmem((length, 2 * length), b16),
            vmem((2 * here, half), b16),
            vmem((2 * here, half), b16),
            vmem((half, 2 * here), b16),
            vmem((2 * here, half), b16),
            vmem((2 * here, half), b16),
            vmem((4, mates, 2, own, here), b16),
            vmem((4, peers, 2, own, here), b16),
            vmem((4, mates, 2, own, here), b16),
            vmem((4, mates, 2, own, here), b16),
            vmem((2, batches, quarter, length), b16),
            vmem((4 * own, 2 * length), f32),
            vmem((4 * own, 2 * length), f32),
            vmem((2 * own, 2 * length), f32),
            vmem((4, 2 * own, 2 * length), b16),
            vmem((2 * own, 2 * length), b16),
            dma((2, peers)),
            dma((2, peers)),
            dma((2,)),
            dma((4, mates)),
            dma((4, mates)),
            dma((4,)),
            dma((batches,)),
            dma((batches,)),
            vmem((3, levels, 2, own, half), f32),
            vmem((3, levels, quarter, half), f32),
            vmem((3, levels, 2, 2 * quarter, half), b16),
            vmem((3, levels, 2, 2 * quarter, half), b16),
            vmem((3, 3, levels, quarter, half), b16),
            vmem((3, 3, levels, quarter, half), b16),
            vmem((3, levels, quarter, half), b16),
            vmem((3, levels, quarter, half), b16),
            vmem((3, batches, quarter, half), b16),
            vmem((2, own, length), f32),
            vmem((2, 2 * quarter, length), f32),
            vmem((2, quarter, length), f32),
            vmem((2, 2 * quarter, length), b16),
            vmem((2, 2 * quarter, length), b16),
            vmem((2, quarter, length), b16),
            vmem((2, quarter, length), b16),
            vmem((quarter, length), b16),
            vmem((quarter, length), b16),
            vmem((batches, quarter, length), b16),
            dma((4,)),
            dma((4,)),
            dma((4, 3)),
            dma((4, 3)),
            dma((4, levels)),
            dma((4, levels)),
            dma((4, batches)),
            dma((4, batches)),
        ],
        compiler_params=pltpu.CompilerParams(
            collective_id=0, has_side_effects=True, vmem_limit_bytes=65900000
        ),
    )(*arguments)
    block, grad_tok, *sums = pl.pallas_call(
        emit,
        out_shape=(
            jax.ShapeDtypeStruct((here, 2 * half), b16),
            jax.ShapeDtypeStruct((here, 2 * half), b16),
            jax.ShapeDtypeStruct((own, half), f32),
            jax.ShapeDtypeStruct((own, half), f32),
            jax.ShapeDtypeStruct((own, half), f32),
            jax.ShapeDtypeStruct((own, length), f32),
        ),
        in_specs=[pl.BlockSpec(memory_space=pltpu.VMEM)] * 4,
        out_specs=(pl.BlockSpec(memory_space=pltpu.VMEM),) * 6,
        compiler_params=pltpu.CompilerParams(vmem_limit_bytes=65900000),
    )(block, grad_tok, weights, filters)
    return (block[None], grad_tok[None], *sums)


def fits(tokens, half):
    peers, batches = lax.axis_size("seq"), lax.axis_size("batch")
    small = (tokens.shape[1] * peers) ** 2 * 4 <= 8 << 20
    square = peers == 8 and batches == 4 and tokens.shape[1] % 128 == 0
    return small and square and half % (16 * batches * peers) == 0


def choose(tokens, *rest):
    short = fits(tokens, rest[0].shape[0])
    return (short_body if short else body)(tokens, *rest)


def solution(mesh):
    in_specs = (P("batch", "seq", None), P(), P(), P(), P("seq", None), P("batch", "seq", None))
    out_specs = (
        P("batch", "seq", None),
        P("batch", "seq", None),
        P("seq", None),
        P("seq", None),
        P("seq", None),
        P("seq", None),
    )
    return jax.shard_map(choose, mesh=mesh, in_specs=in_specs, out_specs=out_specs, check_vma=False)
```

```python
import functools
import math

import jax
import jax.numpy as jnp
import numpy as np
from jax import lax
from jax.experimental import pallas as pl
from jax.experimental.pallas import tpu as pltpu
from jax.sharding import PartitionSpec as P

precise = lax.Precision.HIGH


def swapped(x, axis, stride):
    return lax.ppermute(x, axis, [(i, i ^ 1 << stride) for i in range(lax.axis_size(axis))])


def angle_tables(count_rows, count_cols, period):
    left = lax.broadcasted_iota(jnp.int32, (count_rows, count_cols), 0)
    right = lax.broadcasted_iota(jnp.int32, (count_rows, count_cols), 1)
    turns = left * right % period
    angle = turns.astype(jnp.float32) * (2.0 * math.pi / period)
    return (jnp.cos(angle), jnp.sin(angle))


def rotation(cosines, sines, direction):
    upper = jnp.stack([cosines, direction * sines])
    lower_row = jnp.stack([-direction * sines, cosines])
    return jnp.stack([upper, lower_row])


def split_sizes(length):
    period = 2 * length
    first = 1 << (period.bit_length() - 1 + 1) // 2
    return (first, period // first)


def make_tables(first, second):
    cos_first, sin_first = angle_tables(first, first, first)
    cos_twist, sin_twist = angle_tables(first, second, first * second)
    cos_second, sin_second = angle_tables(second, second, second)
    forward_first = rotation(cos_first, sin_first, 1.0)
    inverse_first = rotation(cos_first, sin_first, -1.0)
    forward_second = rotation(cos_second, sin_second, 1.0)
    inverse_second = rotation(cos_second, sin_second, -1.0)
    return (forward_first, inverse_first, forward_second, inverse_second, cos_twist, sin_twist)


def forward_spectrum(signal, tables, first, second):
    forward_first, inverse_first, forward_second, inverse_second, cos_twist, sin_twist = tables
    lower = first // 2
    folded = signal.reshape(2, signal.shape[1], lower, second)
    section = jnp.einsum("brnm,abnk->arkm", folded, forward_first[:, :, :lower], precision=precise)
    turned = jnp.stack(
        [
            section[0] * cos_twist + section[1] * sin_twist,
            section[1] * cos_twist - section[0] * sin_twist,
        ]
    )
    return jnp.einsum("brkm,abmj->arkj", turned, forward_second, precision=precise)


def inverse_spectrum(spectrum, tables, first, second, both):
    forward_first, inverse_first, forward_second, inverse_second, cos_twist, sin_twist = tables
    lower = first // 2
    rows = spectrum.shape[1]
    inner = jnp.einsum("brkj,abjm->arkm", spectrum, inverse_second, precision=precise)
    turned = jnp.stack(
        [inner[0] * cos_twist - inner[1] * sin_twist, inner[1] * cos_twist + inner[0] * sin_twist]
    )
    if both:
        signal = jnp.einsum(
            "brkm,abkn->arnm", turned, inverse_first[:, :, :, :lower], precision=precise
        )
        return (signal / (first * second)).reshape(2, rows, lower * second)
    signal = jnp.einsum("brkm,bkn->rnm", turned, inverse_first[0][:, :, :lower], precision=precise)
    return (signal / (first * second)).reshape(rows, lower * second)


def complex_product(left, right):
    return jnp.stack(
        [left[0] * right[0] - left[1] * right[1], left[0] * right[1] + left[1] * right[0]]
    )


def conjugate_product(left, right):
    return jnp.stack(
        [left[0] * right[0] + left[1] * right[1], left[0] * right[1] - left[1] * right[0]]
    )


def mirror(array, seq_dim):
    moved = array
    for bit_index in range(lax.axis_size("seq").bit_length() - 1):
        moved = swapped(moved, "seq", bit_index)
    return jnp.flip(moved, axis=seq_dim)


def to_channels(stacked):
    return lax.all_to_all(stacked, "seq", split_axis=1, concat_axis=2, tiled=True)


def to_tokens(stacked):
    return lax.all_to_all(stacked, "seq", split_axis=2, concat_axis=1, tiled=True)


def body(tokens, w_query, w_value, w_out, long_filter, cotangent):
    floats = jnp.float32
    halves = jnp.bfloat16
    half = w_query.shape[0]
    seq_count = lax.axis_size("seq")
    batch_count = lax.axis_size("batch")
    length = tokens.shape[1] * seq_count
    first, second = split_sizes(length)
    tables = make_tables(first, second)
    scale = (2.0 * batch_count * length) ** (-0.5)
    source = tokens[0]
    front = source[:, :half]
    back = source[:, half:]
    back_strand = mirror(back, 0)[:, ::-1]
    strands = jnp.stack([front, back_strand])
    query = jnp.einsum("stk,kh->sht", strands, w_query, preferred_element_type=floats).astype(
        halves
    )
    value = jnp.einsum("stk,kh->sht", strands, w_value, preferred_element_type=floats).astype(
        halves
    )
    value_sig = to_channels(value).astype(floats)
    value_spec = forward_spectrum(value_sig, tables, first, second)
    taps_spec = forward_spectrum(
        jnp.stack([long_filter, jnp.zeros_like(long_filter)]), tables, first, second
    )
    conv_sig = inverse_spectrum(complex_product(value_spec, taps_spec), tables, first, second, True)
    conv_tok = to_tokens(conv_sig.astype(halves))
    gated = (query.astype(floats) * conv_tok.astype(floats)).astype(halves)
    gated_back = mirror(gated[1], 1)
    out_front = jnp.einsum("ht,hk->tk", gated[0], w_out, preferred_element_type=floats)
    out_back = jnp.einsum("ht,hk->tk", gated_back, w_out, preferred_element_type=floats)
    block_out = jnp.concatenate(
        [front.astype(floats) + out_front, back.astype(floats) + out_back[:, ::-1]], axis=1
    ).astype(halves)[None]
    upstream = cotangent[0]
    up_front = upstream[:, :half]
    up_back = upstream[:, half:]
    grad_back = mirror(up_back, 0)[:, ::-1]
    grad_strands = jnp.stack([up_front, grad_back])
    grad_gated = jnp.einsum(
        "stk,hk->sht", grad_strands, w_out, preferred_element_type=floats
    ).astype(halves)
    grad_query_t = (grad_gated.astype(floats) * conv_tok.astype(floats)).astype(halves)
    grad_conv = (grad_gated.astype(floats) * query.astype(floats)).astype(halves)
    grad_sig = to_channels(grad_conv).astype(floats)
    grad_spec = forward_spectrum(grad_sig, tables, first, second)
    value_grad_sig = inverse_spectrum(
        conjugate_product(taps_spec, grad_spec), tables, first, second, True
    )
    filter_part = (
        inverse_spectrum(conjugate_product(value_spec, grad_spec), tables, first, second, False)
        * scale
    )
    grad_value_t = to_tokens(value_grad_sig.astype(halves))
    front_in = jnp.einsum(
        "ht,kh->tk", grad_query_t[0], w_query, preferred_element_type=floats
    ) + jnp.einsum("ht,kh->tk", grad_value_t[0], w_value, preferred_element_type=floats)
    paired = jnp.stack([grad_query_t[1], grad_value_t[1]])
    paired = mirror(paired, 2)
    back_in = jnp.einsum(
        "ht,kh->tk", paired[0], w_query, preferred_element_type=floats
    ) + jnp.einsum("ht,kh->tk", paired[1], w_value, preferred_element_type=floats)
    grad_tokens = jnp.concatenate(
        [up_front.astype(floats) + front_in, up_back.astype(floats) + back_in[:, ::-1]], axis=1
    ).astype(halves)[None]
    term_query = jnp.einsum("stk,sht->kh", strands, grad_query_t, preferred_element_type=floats)
    term_value = jnp.einsum("stk,sht->kh", strands, grad_value_t, preferred_element_type=floats)
    term_out = jnp.einsum("sht,stk->hk", gated, grad_strands, preferred_element_type=floats)
    share = lax.psum_scatter(
        jnp.concatenate([term_query, term_value, term_out], axis=1) * scale,
        "seq",
        scatter_dimension=0,
        tiled=True,
    )
    share, filter_total = (
        lax.psum(share.astype(jnp.bfloat16), "batch").astype(jnp.float32),
        lax.psum(filter_part.astype(jnp.bfloat16), "batch").astype(jnp.float32),
    )
    return (
        block_out,
        grad_tokens,
        share[:, :half],
        share[:, half : 2 * half],
        share[:, 2 * half :],
        filter_total,
    )

MESH = pl.DeviceIdType.MESH


def angle_parts(length):
    step = 1 << (length.bit_length() - 1) // 2
    angle = np.pi * (np.arange(length) + 0.5)[None] / length
    coarse = np.arange(length // step)[:, None] * step * angle
    fine = np.arange(step)[:, None] * angle
    return (
        np.stack([np.cos(coarse), np.sin(coarse)]).astype(np.float32),
        np.stack([np.cos(fine), np.sin(fine)]).astype(np.float32),
    )


def matmul(left, right):
    return jnp.dot(left, right, preferred_element_type=jnp.float32)


def matmul_t(left, right):
    return lax.dot_general(
        left, right, (((1,), (1,)), ((), ())), preferred_element_type=jnp.float32
    )


def times(x, h, conj):
    size = x.shape[1] // 2
    xr, xs, hr, hs = x[:, :size], x[:, size:], h[:, :size], h[:, size:]
    if conj:
        return xr * hr + xs * hs, xs * hr - xr * hs
    return xr * hr - xs * hs, xr * hs + xs * hr


def fused(
    scale,
    tok_in, wq_in, wv_in, wo_in, taps_in, cot_in, coarse_in, fine_in,
    block_out, grad_out, out_w, out_f,
    block, grad_tok, osem,
    tok, wq, wv, wo, taps, cot, coarse, fine, lsem,
    table, strands, ups, strands_t, query, gates, send1, recv1, send2, recv2,
    both_taps, vspec, gspec, hspec, yspec, fspec,
    ssem1, rsem1, lsem1, ssem2, rsem2, lsem2, ssem_t, rsem_t,
    acc, kept, send_a, recv_a, send_b, recv_b, send_c, recv_c, full,
    acc_f, kept_f, last_f, send_af, recv_af, send_bf, recv_bf, send_cf, recv_cf, full_f,
    ssem_a, rsem_a, ssem_b, rsem_b, ssem_c, rsem_c, ssem_d, rsem_d,
):
    peers, batches = lax.axis_size("seq"), lax.axis_size("batch")
    me, seat = lax.axis_index("seq"), lax.axis_index("batch")
    here, half = tok.shape[0], wq.shape[0]
    f32, b16 = jnp.float32, jnp.bfloat16
    own = half // peers
    length = here * peers
    quarter = own // batches
    mates = peers // 2
    wide = mates * here
    rows = 2 * own
    side, seat_in_side = me // mates, lax.rem(me, mates)
    other = 1 - side
    sign = (2 * side - 1).astype(f32)
    column, level = lax.rem(me, 2), me // 2
    levels = peers // 2
    low, high = lax.rem(seat, 2), seat // 2
    slot = 2 * low + high

    barrier = pltpu.get_barrier_semaphore()
    across = me + 1 - 2 * column
    facing = seat + 2 - 4 * high
    for r in range(1, peers):
        pl.semaphore_signal(
            barrier, inc=1, device_id={"seq": lax.rem(me + r, peers)}, device_id_type=MESH
        )
    for r in range(1, batches):
        pl.semaphore_signal(
            barrier, inc=1, device_id={"batch": lax.rem(seat + r, batches)}, device_id_type=MESH
        )
    pl.semaphore_signal(
        barrier, inc=1, device_id={"seq": across, "batch": facing}, device_id_type=MESH
    )
    loads = {}
    pairs = (
        ("tok", tok_in, tok), ("wv", wv_in, wv), ("taps", taps_in, taps), ("cot", cot_in, cot),
        ("wo", wo_in, wo), ("wq", wq_in, wq), ("coarse", coarse_in, coarse), ("fine", fine_in, fine),
    )
    for index, (name, src, dst) in enumerate(pairs):
        loads[name] = pltpu.make_async_copy(src, dst, lsem.at[index])
        loads[name].start()

    def remote(src, dst, ssem, rsem, **device):
        copy = pltpu.make_async_remote_copy(
            src_ref=src, dst_ref=dst, send_sem=ssem, recv_sem=rsem,
            device_id=device, device_id_type=MESH,
        )
        copy.start()
        return copy

    def local(src, dst, sem):
        copy = pltpu.make_async_copy(src, dst, sem)
        copy.start()
        return copy

    def wait(copies):
        for c in copies:
            c.wait()

    flip = (
        lax.broadcasted_iota(jnp.int32, (half, half), 0)
        + lax.broadcasted_iota(jnp.int32, (half, half), 1)
        == half - 1
    ).astype(f32).astype(b16)

    def stage_rows(index, x):
        turned = x.T
        for bh in range(2):
            for bj in range(mates):
                start = (bh * mates + bj) * own
                send1[index, bj, bh] = turned[start : start + own]

    loads["tok"].wait()
    strands[:here] = tok[:, :half]
    strands[here:] = matmul(tok[:, half:], flip).astype(b16)
    loads["wv"].wait()
    value = matmul(strands[...], wv[...]).astype(b16)
    stage_rows(0, value[:here])
    stage_rows(1, value[here:])
    loads["taps"].wait()
    both_taps[pl.ds(side, 1)] = taps[...].astype(b16).reshape(1, batches, quarter, length)
    pl.semaphore_wait(barrier, peers + batches - 1)

    partner = lax.rem(me + mates, peers)
    tap_copy = remote(
        both_taps.at[side, seat], both_taps.at[side, seat], ssem_t.at[0], rsem_t.at[0], seq=partner
    )

    def out1_cross(d):
        c = 2 * d + (side if d == 0 else other)
        copies = []
        for r in range(mates):
            q = lax.rem(seat_in_side + r, mates)
            copies.append(
                remote(
                    send1.at[c, q], recv1.at[c, me], ssem1.at[d, mates + r], rsem1.at[d, mates + r],
                    seq=other * mates + q,
                )
            )
        return copies

    def out1_own(d):
        pair = pl.ds(2 * d, 2)
        copies = []
        for r in range(1, mates):
            q = lax.rem(seat_in_side + r, mates)
            copies.append(
                remote(
                    send1.at[pair, q], recv1.at[pair, me], ssem1.at[d, r], rsem1.at[d, r],
                    seq=side * mates + q,
                )
            )
        copies.append(local(send1.at[pair, seat_in_side], recv1.at[pair, me], lsem1.at[d]))
        return copies

    def out2(k, c):
        copies = []
        for r in range(1, mates):
            q = lax.rem(seat_in_side + r, mates)
            copies.append(
                remote(
                    send2.at[c, q], recv2.at[c, seat_in_side], ssem2.at[k, r], rsem2.at[k, r],
                    seq=side * mates + q,
                )
            )
        copies.append(local(send2.at[c, seat_in_side], recv2.at[c, seat_in_side], lsem2.at[k]))
        return copies

    own_v = out1_own(0)
    cross_v = out1_cross(0)

    for name in ("cot", "wo", "wq"):
        loads[name].wait()
    ups[:here] = cot[:, :half]
    ups[here:] = matmul(cot[:, half:], flip).astype(b16)
    query[...] = matmul(strands[...], wq[...]).astype(b16)
    gates[...] = matmul_t(ups[...], wo[...]).astype(b16)
    grad_conv = (gates[...].astype(f32) * query[...].astype(f32)).astype(b16)
    stage_rows(2, grad_conv[:here])
    stage_rows(3, grad_conv[here:])
    own_g = out1_own(1)
    cross_g = out1_cross(1)

    for name in ("coarse", "fine"):
        loads[name].wait()
    count, step = coarse.shape[1], fine.shape[1]

    @pl.loop(0, count)
    def _(a):
        ca, sa = coarse[0, pl.ds(a, 1), :], coarse[1, pl.ds(a, 1), :]
        at = pl.ds(pl.multiple_of(a * step, step), step)
        table[at, :length] = (ca * fine[0] - sa * fine[1]).astype(b16)
        table[at, length:] = (sa * fine[0] + ca * fine[1]).astype(b16)

    tap_copy.wait()
    tap_copies = [
        remote(
            both_taps.at[other, seat], both_taps.at[other, seat], ssem_t.at[r], rsem_t.at[r],
            batch=lax.rem(seat + r, batches),
        )
        for r in range(1, batches)
    ]
    strands_t[...] = strands[...].T

    def rows_at(i):
        return pl.ds(pl.multiple_of(i * rows, rows), rows)

    def table_of(which):
        return table[pl.ds(pl.multiple_of(which * wide, wide), wide), :]

    def signal(c, which):
        return jnp.concatenate(
            [recv1[c, which * mates + i].reshape(rows, here) for i in range(mates)], axis=1
        )

    def own_signals(d):
        return jnp.concatenate([signal(2 * d, side), signal(2 * d + 1, side)], axis=0)

    def returned(k, c, spec, conj):
        r, s = times(spec, hspec[...], conj)
        yspec[k, :, :length] = r.astype(b16)
        yspec[k, :, length:] = s.astype(b16)
        back = (matmul_t(yspec[k], table_of(side)) * (1.0 / length)).astype(b16)
        for q in range(mates):
            send2[pl.ds(c, 1), q] = back[:, q * here : (q + 1) * here].reshape(1, 2, own, here)
        return out2(k, c)

    def part_of(bit, size):
        return pl.ds(pl.multiple_of(bit * size, size), size)

    def weight(m, product):
        acc[m] = (product * scale).reshape(levels, 2, own, half)

    def stage_a(m):
        send_a[m] = acc[m, :, :, part_of(1 - low, 2 * quarter), :].astype(b16)
        return remote(
            send_a.at[m], recv_a.at[m], ssem_a.at[m], rsem_a.at[m], batch=2 * high + 1 - low
        )

    def stage_b(m, copy):
        copy.wait()

        def pick(x, y):
            at = pl.ds(pl.multiple_of((2 * low + y) * quarter, quarter), quarter)
            mine = acc[m, :, pl.ds(x, 1), at, :]
            theirs = recv_a[m, :, pl.ds(x, 1), part_of(y, quarter), :].astype(f32)
            return (mine + theirs).reshape(levels, quarter, half)

        copies = []
        for index, (dx, dy) in enumerate(((1, 1), (1, 0), (0, 1))):
            x = 1 - column if dx else column
            y = 1 - high if dy else high
            send_b[m, index] = pick(x, y).astype(b16)
            copies.append(
                remote(
                    send_b.at[m, index], recv_b.at[m, index], ssem_b.at[m, index],
                    rsem_b.at[m, index], seq=across if dx else me, batch=facing if dy else seat,
                )
            )
        kept[m] = pick(column, high)
        return copies

    def stage_c(m, copies):
        wait(copies)
        send_c[m] = (kept[m] + jnp.sum(recv_b[m].astype(f32), axis=0)).astype(b16)
        copies = []
        for r in range(1, levels):
            z = lax.rem(level + r, levels)
            copies.append(
                remote(
                    send_c.at[m, z], recv_c.at[m, level], ssem_c.at[m, r], rsem_c.at[m, r],
                    seq=2 * z + column,
                )
            )
        recv_c[m, level] = send_c[m, level]
        return copies

    def share(m, whole):
        return [
            remote(
                whole.at[slot], whole.at[slot], ssem_d.at[m, r], rsem_d.at[m, r],
                batch=lax.rem(seat + r, batches),
            )
            for r in range(1, batches)
        ]

    def stage_d(m, copies):
        wait(copies)
        full[m, slot] = jnp.sum(recv_c[m].astype(f32), axis=0).astype(b16)
        return share(m, full.at[m])

    def leave(index, src, dst):
        return local(src, dst, osem.at[index])

    def finish(m, copies):
        wait(copies)
        return leave(m, full_f if m == 3 else full.at[m], out_f if m == 3 else out_w.at[m])

    def rejoin(c):
        return jnp.concatenate(
            [recv2[c, bj, bh] for bh in range(2) for bj in range(mates)], axis=0
        ).T

    wait(own_v)
    vspec[...] = matmul(own_signals(0), table_of(side))
    wait(tap_copies)
    hspec[...] = matmul(both_taps[...].reshape(rows, length), table[...])
    hspec[:, length:] = hspec[:, length:] * sign
    self_v = returned(0, side, vspec[rows_at(side), :], True)
    wait(cross_v)
    vspec[rows_at(other), :] = vspec[rows_at(other), :] + matmul(
        signal(other, other), table_of(other)
    )
    full_v = returned(1, other, vspec[rows_at(other), :], False)

    wait(own_g)
    gspec[...] = matmul(own_signals(1), table_of(side))
    self_g = returned(2, 2 + other, gspec[rows_at(other), :], True)
    r0, s0 = times(gspec[rows_at(other), :], vspec[rows_at(other), :], True)
    r1, s1 = times(gspec[rows_at(side), :], vspec[rows_at(side), :], True)
    fspec[:, :length] = (r0 + r1).astype(b16)
    fspec[:, length:] = ((s0 - s1) * sign).astype(b16)
    acc_f[...] = (matmul_t(fspec[...], table[...]) * (scale / length)).reshape(2, own, length)
    send_af[...] = acc_f[:, part_of(1 - low, 2 * quarter), :].astype(b16)
    af = remote(send_af, recv_af, ssem_a.at[3], rsem_a.at[3], batch=2 * high + 1 - low)
    af.wait()
    kept_f[...] = acc_f[:, part_of(low, 2 * quarter), :] + recv_af[...].astype(f32)
    send_bf[...] = kept_f[:, part_of(1 - high, quarter), :].astype(b16)
    bf = remote(send_bf, recv_bf, ssem_b.at[3, 0], rsem_b.at[3, 0], batch=facing)
    wait(cross_g)
    gspec[rows_at(side), :] = gspec[rows_at(side), :] + matmul(
        signal(2 + side, other), table_of(other)
    )
    full_g = returned(3, 2 + side, gspec[rows_at(side), :], False)
    wait(self_v)
    wait(full_v)
    conv = jnp.concatenate([rejoin(0), rejoin(1)], axis=0).astype(f32)
    grad_query = (gates[...].astype(f32) * conv).astype(b16)
    weight(0, matmul(strands_t[...], grad_query))
    a0 = stage_a(0)
    gated = (query[...].astype(f32) * conv).astype(b16)
    weight(1, matmul(gated.T, ups[...]))
    a1 = stage_a(1)
    b0 = stage_b(0, a0)
    bf.wait()
    last_f[...] = kept_f[:, part_of(high, quarter), :] + recv_bf[...].astype(f32)
    send_cf[...] = last_f[other].astype(b16)
    cf = remote(send_cf, recv_cf, ssem_c.at[3, 0], rsem_c.at[3, 0], seq=partner)
    b1 = stage_b(1, a1)
    wait(self_g)
    wait(full_g)
    value_0, value_1 = rejoin(2), rejoin(3)
    grad_value = jnp.concatenate([value_0, value_1], axis=0)
    weight(2, matmul(strands_t[...], grad_value))
    a2 = stage_a(2)
    total = strands[...].astype(f32) + matmul(gated, wo[...])
    block[:, :half] = total[:here].astype(b16)
    b2 = stage_b(2, a2)
    block[:, half:] = matmul(total[here:].astype(b16), flip).astype(b16)
    o4 = leave(4, block, block_out)
    c0 = stage_c(0, b0)
    cf.wait()
    full_f[slot] = (last_f[side] + recv_cf[...].astype(f32)).astype(b16)
    df = share(3, full_f)
    c1 = stage_c(1, b1)
    total = ups[...].astype(f32) + matmul_t(grad_query, wq[...]) + matmul_t(grad_value, wv[...])
    grad_tok[:, :half] = total[:here].astype(b16)
    grad_tok[:, half:] = matmul(total[here:].astype(b16), flip).astype(b16)
    o5 = leave(5, grad_tok, grad_out)
    d0 = stage_d(0, c0)
    c2 = stage_c(2, b2)
    d1 = stage_d(1, c1)
    o3 = finish(3, df)
    o0 = finish(0, d0)
    d2 = stage_d(2, c2)
    o1 = finish(1, d1)
    o2 = finish(2, d2)
    wait((o0, o1, o2, o3, o4, o5))


def emit(block, grad_tok, weights, filters, block_out, grad_out, out_q, out_v, out_o, out_f):
    block_out[...] = block[...]
    grad_out[...] = grad_tok[...]
    out_q[...] = weights[0].reshape(out_q.shape).astype(out_q.dtype)
    out_o[...] = weights[1].reshape(out_o.shape).astype(out_o.dtype)
    out_v[...] = weights[2].reshape(out_v.shape).astype(out_v.dtype)
    out_f[...] = filters[...].reshape(out_f.shape).astype(out_f.dtype)


def short_body(tokens, w_query, w_value, w_out, long_filter, cotangent):
    f32, b16 = jnp.float32, jnp.bfloat16
    half = w_query.shape[0]
    peers = lax.axis_size("seq")
    here = tokens.shape[1]
    length = here * peers
    own = half // peers
    scale = (2.0 * lax.axis_size("batch") * length) ** (-0.5)
    coarse, fine = angle_parts(length)
    dma = pltpu.SemaphoreType.DMA
    batches = lax.axis_size("batch")
    quarter = own // batches
    mates = levels = peers // 2
    vmem = pltpu.VMEM
    arguments = (tokens[0], w_query, w_value, w_out, long_filter, cotangent[0], coarse, fine)
    block, grad_tok, weights, filters = pl.pallas_call(
        functools.partial(fused, scale),
        out_shape=(
            jax.ShapeDtypeStruct((here, 2 * half), b16),
            jax.ShapeDtypeStruct((here, 2 * half), b16),
            jax.ShapeDtypeStruct((3, batches, quarter, half), b16),
            jax.ShapeDtypeStruct((batches, quarter, length), b16),
        ),
        in_specs=[pl.BlockSpec(memory_space=pltpu.HBM)] * 8,
        out_specs=(pl.BlockSpec(memory_space=pltpu.HBM),) * 4,
        scratch_shapes=[
            vmem((here, 2 * half), b16),
            vmem((here, 2 * half), b16),
            dma((6,)),
            *(vmem(a.shape, a.dtype) for a in arguments),
            dma((8,)),
            vmem((length, 2 * length), b16),
            vmem((2 * here, half), b16),
            vmem((2 * here, half), b16),
            vmem((half, 2 * here), b16),
            vmem((2 * here, half), b16),
            vmem((2 * here, half), b16),
            vmem((4, mates, 2, own, here), b16),
            vmem((4, peers, 2, own, here), b16),
            vmem((4, mates, 2, own, here), b16),
            vmem((4, mates, 2, own, here), b16),
            vmem((2, batches, quarter, length), b16),
            vmem((4 * own, 2 * length), f32),
            vmem((4 * own, 2 * length), f32),
            vmem((2 * own, 2 * length), f32),
            vmem((4, 2 * own, 2 * length), b16),
            vmem((2 * own, 2 * length), b16),
            dma((2, peers)),
            dma((2, peers)),
            dma((2,)),
            dma((4, mates)),
            dma((4, mates)),
            dma((4,)),
            dma((batches,)),
            dma((batches,)),
            vmem((3, levels, 2, own, half), f32),
            vmem((3, levels, quarter, half), f32),
            vmem((3, levels, 2, 2 * quarter, half), b16),
            vmem((3, levels, 2, 2 * quarter, half), b16),
            vmem((3, 3, levels, quarter, half), b16),
            vmem((3, 3, levels, quarter, half), b16),
            vmem((3, levels, quarter, half), b16),
            vmem((3, levels, quarter, half), b16),
            vmem((3, batches, quarter, half), b16),
            vmem((2, own, length), f32),
            vmem((2, 2 * quarter, length), f32),
            vmem((2, quarter, length), f32),
            vmem((2, 2 * quarter, length), b16),
            vmem((2, 2 * quarter, length), b16),
            vmem((2, quarter, length), b16),
            vmem((2, quarter, length), b16),
            vmem((quarter, length), b16),
            vmem((quarter, length), b16),
            vmem((batches, quarter, length), b16),
            dma((4,)),
            dma((4,)),
            dma((4, 3)),
            dma((4, 3)),
            dma((4, levels)),
            dma((4, levels)),
            dma((4, batches)),
            dma((4, batches)),
        ],
        compiler_params=pltpu.CompilerParams(
            collective_id=0, has_side_effects=True, vmem_limit_bytes=65900000
        ),
    )(*arguments)
    block, grad_tok, *sums = pl.pallas_call(
        emit,
        out_shape=(
            jax.ShapeDtypeStruct((here, 2 * half), b16),
            jax.ShapeDtypeStruct((here, 2 * half), b16),
            jax.ShapeDtypeStruct((own, half), f32),
            jax.ShapeDtypeStruct((own, half), f32),
            jax.ShapeDtypeStruct((own, half), f32),
            jax.ShapeDtypeStruct((own, length), f32),
        ),
        in_specs=[pl.BlockSpec(memory_space=pltpu.VMEM)] * 4,
        out_specs=(pl.BlockSpec(memory_space=pltpu.VMEM),) * 6,
        compiler_params=pltpu.CompilerParams(vmem_limit_bytes=65900000),
    )(block, grad_tok, weights, filters)
    return (block[None], grad_tok[None], *sums)


def fits(tokens, half):
    peers, batches = lax.axis_size("seq"), lax.axis_size("batch")
    small = (tokens.shape[1] * peers) ** 2 * 4 <= 8 << 20
    square = peers == 8 and batches == 4 and tokens.shape[1] % 128 == 0
    return small and square and half % (16 * batches * peers) == 0


def choose(tokens, *rest):
    short = fits(tokens, rest[0].shape[0])
    return (short_body if short else body)(tokens, *rest)


def solution(mesh):
    in_specs = (P("batch", "seq", None), P(), P(), P(), P("seq", None), P("batch", "seq", None))
    out_specs = (
        P("batch", "seq", None),
        P("batch", "seq", None),
        P("seq", None),
        P("seq", None),
        P("seq", None),
        P("seq", None),
    )
    return jax.shard_map(choose, mesh=mesh, in_specs=in_specs, out_specs=out_specs, check_vma=False)
```

```python
import functools
import math

import jax
import jax.numpy as jnp
import numpy as np
from jax import lax
from jax.experimental import pallas as pl
from jax.experimental.pallas import tpu as pltpu
from jax.sharding import PartitionSpec as P

precise = lax.Precision.HIGH


def swapped(x, axis, stride):
    return lax.ppermute(x, axis, [(i, i ^ 1 << stride) for i in range(lax.axis_size(axis))])


def angle_tables(count_rows, count_cols, period):
    left = lax.broadcasted_iota(jnp.int32, (count_rows, count_cols), 0)
    right = lax.broadcasted_iota(jnp.int32, (count_rows, count_cols), 1)
    turns = left * right % period
    angle = turns.astype(jnp.float32) * (2.0 * math.pi / period)
    return (jnp.cos(angle), jnp.sin(angle))


def rotation(cosines, sines, direction):
    upper = jnp.stack([cosines, direction * sines])
    lower_row = jnp.stack([-direction * sines, cosines])
    return jnp.stack([upper, lower_row])


def split_sizes(length):
    period = 2 * length
    first = 1 << (period.bit_length() - 1 + 1) // 2
    return (first, period // first)


def make_tables(first, second):
    cos_first, sin_first = angle_tables(first, first, first)
    cos_twist, sin_twist = angle_tables(first, second, first * second)
    cos_second, sin_second = angle_tables(second, second, second)
    forward_first = rotation(cos_first, sin_first, 1.0)
    inverse_first = rotation(cos_first, sin_first, -1.0)
    forward_second = rotation(cos_second, sin_second, 1.0)
    inverse_second = rotation(cos_second, sin_second, -1.0)
    return (forward_first, inverse_first, forward_second, inverse_second, cos_twist, sin_twist)


def forward_spectrum(signal, tables, first, second):
    forward_first, inverse_first, forward_second, inverse_second, cos_twist, sin_twist = tables
    lower = first // 2
    folded = signal.reshape(2, signal.shape[1], lower, second)
    section = jnp.einsum("brnm,abnk->arkm", folded, forward_first[:, :, :lower], precision=precise)
    turned = jnp.stack(
        [
            section[0] * cos_twist + section[1] * sin_twist,
            section[1] * cos_twist - section[0] * sin_twist,
        ]
    )
    return jnp.einsum("brkm,abmj->arkj", turned, forward_second, precision=precise)


def inverse_spectrum(spectrum, tables, first, second, both):
    forward_first, inverse_first, forward_second, inverse_second, cos_twist, sin_twist = tables
    lower = first // 2
    rows = spectrum.shape[1]
    inner = jnp.einsum("brkj,abjm->arkm", spectrum, inverse_second, precision=precise)
    turned = jnp.stack(
        [inner[0] * cos_twist - inner[1] * sin_twist, inner[1] * cos_twist + inner[0] * sin_twist]
    )
    if both:
        signal = jnp.einsum(
            "brkm,abkn->arnm", turned, inverse_first[:, :, :, :lower], precision=precise
        )
        return (signal / (first * second)).reshape(2, rows, lower * second)
    signal = jnp.einsum("brkm,bkn->rnm", turned, inverse_first[0][:, :, :lower], precision=precise)
    return (signal / (first * second)).reshape(rows, lower * second)


def complex_product(left, right):
    return jnp.stack(
        [left[0] * right[0] - left[1] * right[1], left[0] * right[1] + left[1] * right[0]]
    )


def conjugate_product(left, right):
    return jnp.stack(
        [left[0] * right[0] + left[1] * right[1], left[0] * right[1] - left[1] * right[0]]
    )


def mirror(array, seq_dim):
    moved = array
    for bit_index in range(lax.axis_size("seq").bit_length() - 1):
        moved = swapped(moved, "seq", bit_index)
    return jnp.flip(moved, axis=seq_dim)


def to_channels(stacked):
    return lax.all_to_all(stacked, "seq", split_axis=1, concat_axis=2, tiled=True)


def to_tokens(stacked):
    return lax.all_to_all(stacked, "seq", split_axis=2, concat_axis=1, tiled=True)


def body(tokens, w_query, w_value, w_out, long_filter, cotangent):
    floats = jnp.float32
    halves = jnp.bfloat16
    half = w_query.shape[0]
    seq_count = lax.axis_size("seq")
    batch_count = lax.axis_size("batch")
    length = tokens.shape[1] * seq_count
    first, second = split_sizes(length)
    tables = make_tables(first, second)
    scale = (2.0 * batch_count * length) ** (-0.5)
    source = tokens[0]
    front = source[:, :half]
    back = source[:, half:]
    back_strand = mirror(back, 0)[:, ::-1]
    strands = jnp.stack([front, back_strand])
    query = jnp.einsum("stk,kh->sht", strands, w_query, preferred_element_type=floats).astype(
        halves
    )
    value = jnp.einsum("stk,kh->sht", strands, w_value, preferred_element_type=floats).astype(
        halves
    )
    value_sig = to_channels(value).astype(floats)
    value_spec = forward_spectrum(value_sig, tables, first, second)
    taps_spec = forward_spectrum(
        jnp.stack([long_filter, jnp.zeros_like(long_filter)]), tables, first, second
    )
    conv_sig = inverse_spectrum(complex_product(value_spec, taps_spec), tables, first, second, True)
    conv_tok = to_tokens(conv_sig.astype(halves))
    gated = (query.astype(floats) * conv_tok.astype(floats)).astype(halves)
    gated_back = mirror(gated[1], 1)
    out_front = jnp.einsum("ht,hk->tk", gated[0], w_out, preferred_element_type=floats)
    out_back = jnp.einsum("ht,hk->tk", gated_back, w_out, preferred_element_type=floats)
    block_out = jnp.concatenate(
        [front.astype(floats) + out_front, back.astype(floats) + out_back[:, ::-1]], axis=1
    ).astype(halves)[None]
    upstream = cotangent[0]
    up_front = upstream[:, :half]
    up_back = upstream[:, half:]
    grad_back = mirror(up_back, 0)[:, ::-1]
    grad_strands = jnp.stack([up_front, grad_back])
    grad_gated = jnp.einsum(
        "stk,hk->sht", grad_strands, w_out, preferred_element_type=floats
    ).astype(halves)
    grad_query_t = (grad_gated.astype(floats) * conv_tok.astype(floats)).astype(halves)
    grad_conv = (grad_gated.astype(floats) * query.astype(floats)).astype(halves)
    grad_sig = to_channels(grad_conv).astype(floats)
    grad_spec = forward_spectrum(grad_sig, tables, first, second)
    value_grad_sig = inverse_spectrum(
        conjugate_product(taps_spec, grad_spec), tables, first, second, True
    )
    filter_part = (
        inverse_spectrum(conjugate_product(value_spec, grad_spec), tables, first, second, False)
        * scale
    )
    grad_value_t = to_tokens(value_grad_sig.astype(halves))
    front_in = jnp.einsum(
        "ht,kh->tk", grad_query_t[0], w_query, preferred_element_type=floats
    ) + jnp.einsum("ht,kh->tk", grad_value_t[0], w_value, preferred_element_type=floats)
    paired = jnp.stack([grad_query_t[1], grad_value_t[1]])
    paired = mirror(paired, 2)
    back_in = jnp.einsum(
        "ht,kh->tk", paired[0], w_query, preferred_element_type=floats
    ) + jnp.einsum("ht,kh->tk", paired[1], w_value, preferred_element_type=floats)
    grad_tokens = jnp.concatenate(
        [up_front.astype(floats) + front_in, up_back.astype(floats) + back_in[:, ::-1]], axis=1
    ).astype(halves)[None]
    term_query = jnp.einsum("stk,sht->kh", strands, grad_query_t, preferred_element_type=floats)
    term_value = jnp.einsum("stk,sht->kh", strands, grad_value_t, preferred_element_type=floats)
    term_out = jnp.einsum("sht,stk->hk", gated, grad_strands, preferred_element_type=floats)
    share = lax.psum_scatter(
        jnp.concatenate([term_query, term_value, term_out], axis=1) * scale,
        "seq",
        scatter_dimension=0,
        tiled=True,
    )
    share, filter_total = (
        lax.psum(share.astype(jnp.bfloat16), "batch").astype(jnp.float32),
        lax.psum(filter_part.astype(jnp.bfloat16), "batch").astype(jnp.float32),
    )
    return (
        block_out,
        grad_tokens,
        share[:, :half],
        share[:, half : 2 * half],
        share[:, 2 * half :],
        filter_total,
    )

MESH = pl.DeviceIdType.MESH


def angle_parts(length):
    step = 1 << (length.bit_length() - 1) // 2
    angle = np.pi * (np.arange(length) + 0.5)[None] / length
    coarse = np.arange(length // step)[:, None] * step * angle
    fine = np.arange(step)[:, None] * angle
    return (
        np.stack([np.cos(coarse), np.sin(coarse)]).astype(np.float32),
        np.stack([np.cos(fine), np.sin(fine)]).astype(np.float32),
    )


def matmul(left, right):
    return jnp.dot(left, right, preferred_element_type=jnp.float32)


def matmul_t(left, right):
    return lax.dot_general(
        left, right, (((1,), (1,)), ((), ())), preferred_element_type=jnp.float32
    )


def times(x, h, conj):
    size = x.shape[1] // 2
    xr, xs, hr, hs = x[:, :size], x[:, size:], h[:, :size], h[:, size:]
    if conj:
        return xr * hr + xs * hs, xs * hr - xr * hs
    return xr * hr - xs * hs, xr * hs + xs * hr


def fused(
    scale,
    tok_in, wq_in, wv_in, wo_in, taps_in, cot_in, coarse_in, fine_in,
    block_out, grad_out, out_w, out_f,
    tok, wq, wv, wo, taps, cot, coarse, fine, lsem,
    table, strands, ups, strands_t, query, gates, send1, recv1, send2, recv2,
    both_taps, vspec, gspec, hspec, yspec, fspec,
    ssem1, rsem1, lsem1, ssem2, rsem2, lsem2, ssem_t, rsem_t,
    acc, kept, send_a, recv_a, send_b, recv_b, send_c, recv_c,
    acc_f, kept_f, last_f, send_af, recv_af, send_bf, recv_bf, send_cf, recv_cf,
    ssem_a, rsem_a, ssem_b, rsem_b, ssem_c, rsem_c, ssem_d, rsem_d,
):
    peers, batches = lax.axis_size("seq"), lax.axis_size("batch")
    me, seat = lax.axis_index("seq"), lax.axis_index("batch")
    here, half = tok.shape[0], wq.shape[0]
    f32, b16 = jnp.float32, jnp.bfloat16
    own = half // peers
    length = here * peers
    quarter = own // batches
    mates = peers // 2
    wide = mates * here
    rows = 2 * own
    side, seat_in_side = me // mates, lax.rem(me, mates)
    other = 1 - side
    sign = (2 * side - 1).astype(f32)
    column, level = lax.rem(me, 2), me // 2
    levels = peers // 2
    low, high = lax.rem(seat, 2), seat // 2
    slot = 2 * low + high

    barrier = pltpu.get_barrier_semaphore()
    across = me + 1 - 2 * column
    facing = seat + 2 - 4 * high
    for r in range(1, peers):
        pl.semaphore_signal(
            barrier, inc=1, device_id={"seq": lax.rem(me + r, peers)}, device_id_type=MESH
        )
    for r in range(1, batches):
        pl.semaphore_signal(
            barrier, inc=1, device_id={"batch": lax.rem(seat + r, batches)}, device_id_type=MESH
        )
    pl.semaphore_signal(
        barrier, inc=1, device_id={"seq": across, "batch": facing}, device_id_type=MESH
    )
    loads = {}
    pairs = (
        ("tok", tok_in, tok), ("wv", wv_in, wv), ("taps", taps_in, taps), ("cot", cot_in, cot),
        ("wo", wo_in, wo), ("wq", wq_in, wq), ("coarse", coarse_in, coarse), ("fine", fine_in, fine),
    )
    for index, (name, src, dst) in enumerate(pairs):
        loads[name] = pltpu.make_async_copy(src, dst, lsem.at[index])
        loads[name].start()

    def remote(src, dst, ssem, rsem, **device):
        copy = pltpu.make_async_remote_copy(
            src_ref=src, dst_ref=dst, send_sem=ssem, recv_sem=rsem,
            device_id=device, device_id_type=MESH,
        )
        copy.start()
        return copy

    def local(src, dst, sem):
        copy = pltpu.make_async_copy(src, dst, sem)
        copy.start()
        return copy

    def wait(copies):
        for c in copies:
            c.wait()

    flip = (
        lax.broadcasted_iota(jnp.int32, (half, half), 0)
        + lax.broadcasted_iota(jnp.int32, (half, half), 1)
        == half - 1
    ).astype(f32).astype(b16)

    def stage_rows(index, x):
        turned = x.T
        for bh in range(2):
            for bj in range(mates):
                start = (bh * mates + bj) * own
                send1[index, bj, bh] = turned[start : start + own]

    loads["tok"].wait()
    strands[:here] = tok[:, :half]
    strands[here:] = matmul(tok[:, half:], flip).astype(b16)
    loads["wv"].wait()
    value = matmul(strands[...], wv[...]).astype(b16)
    stage_rows(0, value[:here])
    stage_rows(1, value[here:])
    loads["taps"].wait()
    both_taps[pl.ds(side, 1)] = taps[...].astype(b16).reshape(1, batches, quarter, length)
    pl.semaphore_wait(barrier, peers + batches - 1)

    partner = lax.rem(me + mates, peers)
    tap_copy = remote(
        both_taps.at[side, seat], both_taps.at[side, seat], ssem_t.at[0], rsem_t.at[0], seq=partner
    )

    def out1_cross(d):
        c = 2 * d + (side if d == 0 else other)
        copies = []
        for r in range(mates):
            q = lax.rem(seat_in_side + r, mates)
            copies.append(
                remote(
                    send1.at[c, q], recv1.at[c, me], ssem1.at[d, mates + r], rsem1.at[d, mates + r],
                    seq=other * mates + q,
                )
            )
        return copies

    def out1_own(d):
        pair = pl.ds(2 * d, 2)
        copies = []
        for r in range(1, mates):
            q = lax.rem(seat_in_side + r, mates)
            copies.append(
                remote(
                    send1.at[pair, q], recv1.at[pair, me], ssem1.at[d, r], rsem1.at[d, r],
                    seq=side * mates + q,
                )
            )
        copies.append(local(send1.at[pair, seat_in_side], recv1.at[pair, me], lsem1.at[d]))
        return copies

    def out2(k, c):
        copies = []
        for r in range(1, mates):
            q = lax.rem(seat_in_side + r, mates)
            copies.append(
                remote(
                    send2.at[c, q], recv2.at[c, seat_in_side], ssem2.at[k, r], rsem2.at[k, r],
                    seq=side * mates + q,
                )
            )
        copies.append(local(send2.at[c, seat_in_side], recv2.at[c, seat_in_side], lsem2.at[k]))
        return copies

    own_v = out1_own(0)
    cross_v = out1_cross(0)

    for name in ("cot", "wo", "wq"):
        loads[name].wait()
    ups[:here] = cot[:, :half]
    ups[here:] = matmul(cot[:, half:], flip).astype(b16)
    query[...] = matmul(strands[...], wq[...]).astype(b16)
    gates[...] = matmul_t(ups[...], wo[...]).astype(b16)
    grad_conv = (gates[...].astype(f32) * query[...].astype(f32)).astype(b16)
    stage_rows(2, grad_conv[:here])
    stage_rows(3, grad_conv[here:])
    own_g = out1_own(1)
    cross_g = out1_cross(1)

    for name in ("coarse", "fine"):
        loads[name].wait()
    count, step = coarse.shape[1], fine.shape[1]

    @pl.loop(0, count)
    def _(a):
        ca, sa = coarse[0, pl.ds(a, 1), :], coarse[1, pl.ds(a, 1), :]
        at = pl.ds(pl.multiple_of(a * step, step), step)
        table[at, :length] = (ca * fine[0] - sa * fine[1]).astype(b16)
        table[at, length:] = (sa * fine[0] + ca * fine[1]).astype(b16)

    tap_copy.wait()
    tap_copies = [
        remote(
            both_taps.at[other, seat], both_taps.at[other, seat], ssem_t.at[r], rsem_t.at[r],
            batch=lax.rem(seat + r, batches),
        )
        for r in range(1, batches)
    ]
    strands_t[...] = strands[...].T

    def rows_at(i):
        return pl.ds(pl.multiple_of(i * rows, rows), rows)

    def table_of(which):
        return table[pl.ds(pl.multiple_of(which * wide, wide), wide), :]

    def signal(c, which):
        return jnp.concatenate(
            [recv1[c, which * mates + i].reshape(rows, here) for i in range(mates)], axis=1
        )

    def own_signals(d):
        return jnp.concatenate([signal(2 * d, side), signal(2 * d + 1, side)], axis=0)

    def returned(k, c, spec, conj):
        r, s = times(spec, hspec[...], conj)
        yspec[k, :, :length] = r.astype(b16)
        yspec[k, :, length:] = s.astype(b16)
        back = (matmul_t(yspec[k], table_of(side)) * (1.0 / length)).astype(b16)
        for q in range(mates):
            send2[pl.ds(c, 1), q] = back[:, q * here : (q + 1) * here].reshape(1, 2, own, here)
        return out2(k, c)

    def part_of(bit, size):
        return pl.ds(pl.multiple_of(bit * size, size), size)

    def weight(m, product):
        acc[m] = (product * scale).reshape(levels, 2, own, half)

    def stage_a(m):
        send_a[m] = acc[m, :, :, part_of(1 - low, 2 * quarter), :].astype(b16)
        return remote(
            send_a.at[m], recv_a.at[m], ssem_a.at[m], rsem_a.at[m], batch=2 * high + 1 - low
        )

    def stage_b(m, copy):
        copy.wait()

        def pick(x, y):
            at = pl.ds(pl.multiple_of((2 * low + y) * quarter, quarter), quarter)
            mine = acc[m, :, pl.ds(x, 1), at, :]
            theirs = recv_a[m, :, pl.ds(x, 1), part_of(y, quarter), :].astype(f32)
            return (mine + theirs).reshape(levels, quarter, half)

        copies = []
        for index, (dx, dy) in enumerate(((1, 1), (1, 0), (0, 1))):
            x = 1 - column if dx else column
            y = 1 - high if dy else high
            send_b[m, index] = pick(x, y).astype(b16)
            copies.append(
                remote(
                    send_b.at[m, index], recv_b.at[m, index], ssem_b.at[m, index],
                    rsem_b.at[m, index], seq=across if dx else me, batch=facing if dy else seat,
                )
            )
        kept[m] = pick(column, high)
        return copies

    def stage_c(m, copies):
        wait(copies)
        send_c[m] = (kept[m] + jnp.sum(recv_b[m].astype(f32), axis=0)).astype(b16)
        copies = []
        for r in range(1, levels):
            z = lax.rem(level + r, levels)
            copies.append(
                remote(
                    send_c.at[m, z], recv_c.at[m, level], ssem_c.at[m, r], rsem_c.at[m, r],
                    seq=2 * z + column,
                )
            )
        recv_c[m, level] = send_c[m, level]
        return copies

    def share(m, whole):
        return [
            remote(
                whole.at[slot], whole.at[slot], ssem_d.at[m, r], rsem_d.at[m, r],
                batch=lax.rem(seat + r, batches),
            )
            for r in range(1, batches)
        ]

    def stage_d(m, copies):
        wait(copies)
        out_w[m, slot] = jnp.sum(recv_c[m].astype(f32), axis=0).astype(b16)
        return share(m, out_w.at[m])

    def rejoin(c):
        return jnp.concatenate(
            [recv2[c, bj, bh] for bh in range(2) for bj in range(mates)], axis=0
        ).T

    wait(own_v)
    vspec[...] = matmul(own_signals(0), table_of(side))
    wait(tap_copies)
    hspec[...] = matmul(both_taps[...].reshape(rows, length), table[...])
    hspec[:, length:] = hspec[:, length:] * sign
    self_v = returned(0, side, vspec[rows_at(side), :], True)
    wait(cross_v)
    vspec[rows_at(other), :] = vspec[rows_at(other), :] + matmul(
        signal(other, other), table_of(other)
    )
    full_v = returned(1, other, vspec[rows_at(other), :], False)

    wait(own_g)
    gspec[...] = matmul(own_signals(1), table_of(side))
    self_g = returned(2, 2 + other, gspec[rows_at(other), :], True)
    r0, s0 = times(gspec[rows_at(other), :], vspec[rows_at(other), :], True)
    r1, s1 = times(gspec[rows_at(side), :], vspec[rows_at(side), :], True)
    fspec[:, :length] = (r0 + r1).astype(b16)
    fspec[:, length:] = ((s0 - s1) * sign).astype(b16)
    acc_f[...] = (matmul_t(fspec[...], table[...]) * (scale / length)).reshape(2, own, length)
    send_af[...] = acc_f[:, part_of(1 - low, 2 * quarter), :].astype(b16)
    af = remote(send_af, recv_af, ssem_a.at[3], rsem_a.at[3], batch=2 * high + 1 - low)
    af.wait()
    kept_f[...] = acc_f[:, part_of(low, 2 * quarter), :] + recv_af[...].astype(f32)
    send_bf[...] = kept_f[:, part_of(1 - high, quarter), :].astype(b16)
    bf = remote(send_bf, recv_bf, ssem_b.at[3, 0], rsem_b.at[3, 0], batch=facing)
    wait(cross_g)
    gspec[rows_at(side), :] = gspec[rows_at(side), :] + matmul(
        signal(2 + side, other), table_of(other)
    )
    full_g = returned(3, 2 + side, gspec[rows_at(side), :], False)
    wait(self_v)
    wait(full_v)
    conv = jnp.concatenate([rejoin(0), rejoin(1)], axis=0).astype(f32)
    grad_query = (gates[...].astype(f32) * conv).astype(b16)
    weight(0, matmul(strands_t[...], grad_query))
    a0 = stage_a(0)
    gated = (query[...].astype(f32) * conv).astype(b16)
    weight(1, matmul(gated.T, ups[...]))
    a1 = stage_a(1)
    b0 = stage_b(0, a0)
    bf.wait()
    last_f[...] = kept_f[:, part_of(high, quarter), :] + recv_bf[...].astype(f32)
    send_cf[...] = last_f[other].astype(b16)
    cf = remote(send_cf, recv_cf, ssem_c.at[3, 0], rsem_c.at[3, 0], seq=partner)
    b1 = stage_b(1, a1)
    wait(self_g)
    wait(full_g)
    value_0, value_1 = rejoin(2), rejoin(3)
    grad_value = jnp.concatenate([value_0, value_1], axis=0)
    weight(2, matmul(strands_t[...], grad_value))
    a2 = stage_a(2)
    total = strands[...].astype(f32) + matmul(gated, wo[...])
    block_out[:, :half] = total[:here].astype(b16)
    b2 = stage_b(2, a2)
    block_out[:, half:] = matmul(total[here:].astype(b16), flip).astype(b16)
    c0 = stage_c(0, b0)
    cf.wait()
    out_f[slot] = (last_f[side] + recv_cf[...].astype(f32)).astype(b16)
    df = share(3, out_f)
    c1 = stage_c(1, b1)
    total = ups[...].astype(f32) + matmul_t(grad_query, wq[...]) + matmul_t(grad_value, wv[...])
    grad_out[:, :half] = total[:here].astype(b16)
    grad_out[:, half:] = matmul(total[here:].astype(b16), flip).astype(b16)
    d0 = stage_d(0, c0)
    c2 = stage_c(2, b2)
    d1 = stage_d(1, c1)
    wait(df)
    wait(d0)
    d2 = stage_d(2, c2)
    wait(d1)
    wait(d2)


def emit(
    block, grad_tok, weights, filters,
    block_out, grad_out, out_q, out_v, out_o, out_f,
    wide_w, wide_f, sem,
):
    copies = []

    def leave(src, dst):
        copy = pltpu.make_async_copy(src, dst, sem.at[len(copies)])
        copy.start()
        copies.append(copy)

    leave(block, block_out)
    leave(grad_tok, grad_out)
    wide_f[...] = filters[...].reshape(wide_f.shape).astype(wide_f.dtype)
    leave(wide_f, out_f)
    for m, dst in enumerate((out_q, out_o, out_v)):
        wide_w[m] = weights[m].reshape(dst.shape).astype(wide_w.dtype)
        leave(wide_w.at[m], dst)
    for copy in copies:
        copy.wait()


def short_body(tokens, w_query, w_value, w_out, long_filter, cotangent):
    f32, b16 = jnp.float32, jnp.bfloat16
    half = w_query.shape[0]
    peers = lax.axis_size("seq")
    here = tokens.shape[1]
    length = here * peers
    own = half // peers
    scale = (2.0 * lax.axis_size("batch") * length) ** (-0.5)
    coarse, fine = angle_parts(length)
    dma = pltpu.SemaphoreType.DMA
    batches = lax.axis_size("batch")
    quarter = own // batches
    mates = levels = peers // 2
    vmem = pltpu.VMEM
    arguments = (tokens[0], w_query, w_value, w_out, long_filter, cotangent[0], coarse, fine)
    block, grad_tok, weights, filters = pl.pallas_call(
        functools.partial(fused, scale),
        out_shape=(
            vmem((here, 2 * half), b16),
            vmem((here, 2 * half), b16),
            vmem((3, batches, quarter, half), b16),
            vmem((batches, quarter, length), b16),
        ),
        in_specs=[pl.BlockSpec(memory_space=pltpu.HBM)] * 8,
        out_specs=(pl.BlockSpec(memory_space=pltpu.VMEM),) * 4,
        scratch_shapes=[
            *(vmem(a.shape, a.dtype) for a in arguments),
            dma((8,)),
            vmem((length, 2 * length), b16),
            vmem((2 * here, half), b16),
            vmem((2 * here, half), b16),
            vmem((half, 2 * here), b16),
            vmem((2 * here, half), b16),
            vmem((2 * here, half), b16),
            vmem((4, mates, 2, own, here), b16),
            vmem((4, peers, 2, own, here), b16),
            vmem((4, mates, 2, own, here), b16),
            vmem((4, mates, 2, own, here), b16),
            vmem((2, batches, quarter, length), b16),
            vmem((4 * own, 2 * length), f32),
            vmem((4 * own, 2 * length), f32),
            vmem((2 * own, 2 * length), f32),
            vmem((4, 2 * own, 2 * length), b16),
            vmem((2 * own, 2 * length), b16),
            dma((2, peers)),
            dma((2, peers)),
            dma((2,)),
            dma((4, mates)),
            dma((4, mates)),
            dma((4,)),
            dma((batches,)),
            dma((batches,)),
            vmem((3, levels, 2, own, half), f32),
            vmem((3, levels, quarter, half), f32),
            vmem((3, levels, 2, 2 * quarter, half), b16),
            vmem((3, levels, 2, 2 * quarter, half), b16),
            vmem((3, 3, levels, quarter, half), b16),
            vmem((3, 3, levels, quarter, half), b16),
            vmem((3, levels, quarter, half), b16),
            vmem((3, levels, quarter, half), b16),
            vmem((2, own, length), f32),
            vmem((2, 2 * quarter, length), f32),
            vmem((2, quarter, length), f32),
            vmem((2, 2 * quarter, length), b16),
            vmem((2, 2 * quarter, length), b16),
            vmem((2, quarter, length), b16),
            vmem((2, quarter, length), b16),
            vmem((quarter, length), b16),
            vmem((quarter, length), b16),
            dma((4,)),
            dma((4,)),
            dma((4, 3)),
            dma((4, 3)),
            dma((4, levels)),
            dma((4, levels)),
            dma((4, batches)),
            dma((4, batches)),
        ],
        compiler_params=pltpu.CompilerParams(
            collective_id=0, has_side_effects=True, vmem_limit_bytes=65900000
        ),
    )(*arguments)
    block, grad_tok, *sums = pl.pallas_call(
        emit,
        out_shape=(
            jax.ShapeDtypeStruct((here, 2 * half), b16),
            jax.ShapeDtypeStruct((here, 2 * half), b16),
            jax.ShapeDtypeStruct((own, half), f32),
            jax.ShapeDtypeStruct((own, half), f32),
            jax.ShapeDtypeStruct((own, half), f32),
            jax.ShapeDtypeStruct((own, length), f32),
        ),
        in_specs=[pl.BlockSpec(memory_space=pltpu.VMEM)] * 4,
        out_specs=(pl.BlockSpec(memory_space=pltpu.HBM),) * 6,
        scratch_shapes=[vmem((3, own, half), f32), vmem((own, length), f32), dma((6,))],
        compiler_params=pltpu.CompilerParams(vmem_limit_bytes=8000000),
    )(block, grad_tok, weights, filters)
    return (block[None], grad_tok[None], *sums)


def fits(tokens, half):
    peers, batches = lax.axis_size("seq"), lax.axis_size("batch")
    small = (tokens.shape[1] * peers) ** 2 * 4 <= 8 << 20
    square = peers == 8 and batches == 4 and tokens.shape[1] % 128 == 0
    return small and square and half % (16 * batches * peers) == 0


def choose(tokens, *rest):
    short = fits(tokens, rest[0].shape[0])
    return (short_body if short else body)(tokens, *rest)


def solution(mesh):
    in_specs = (P("batch", "seq", None), P(), P(), P(), P("seq", None), P("batch", "seq", None))
    out_specs = (
        P("batch", "seq", None),
        P("batch", "seq", None),
        P("seq", None),
        P("seq", None),
        P("seq", None),
        P("seq", None),
    )
    return jax.shard_map(choose, mesh=mesh, in_specs=in_specs, out_specs=out_specs, check_vma=False)
```

```python
import functools
import math

import jax
import jax.numpy as jnp
import numpy as np
from jax import lax
from jax.experimental import pallas as pl
from jax.experimental.pallas import tpu as pltpu
from jax.sharding import PartitionSpec as P

precise = lax.Precision.HIGH


def swapped(x, axis, stride):
    return lax.ppermute(x, axis, [(i, i ^ 1 << stride) for i in range(lax.axis_size(axis))])


def angle_tables(count_rows, count_cols, period):
    left = lax.broadcasted_iota(jnp.int32, (count_rows, count_cols), 0)
    right = lax.broadcasted_iota(jnp.int32, (count_rows, count_cols), 1)
    turns = left * right % period
    angle = turns.astype(jnp.float32) * (2.0 * math.pi / period)
    return (jnp.cos(angle), jnp.sin(angle))


def rotation(cosines, sines, direction):
    upper = jnp.stack([cosines, direction * sines])
    lower_row = jnp.stack([-direction * sines, cosines])
    return jnp.stack([upper, lower_row])


def split_sizes(length):
    period = 2 * length
    first = 1 << (period.bit_length() - 1 + 1) // 2
    return (first, period // first)


def make_tables(first, second):
    cos_first, sin_first = angle_tables(first, first, first)
    cos_twist, sin_twist = angle_tables(first, second, first * second)
    cos_second, sin_second = angle_tables(second, second, second)
    forward_first = rotation(cos_first, sin_first, 1.0)
    inverse_first = rotation(cos_first, sin_first, -1.0)
    forward_second = rotation(cos_second, sin_second, 1.0)
    inverse_second = rotation(cos_second, sin_second, -1.0)
    return (forward_first, inverse_first, forward_second, inverse_second, cos_twist, sin_twist)


def forward_spectrum(signal, tables, first, second):
    forward_first, inverse_first, forward_second, inverse_second, cos_twist, sin_twist = tables
    lower = first // 2
    folded = signal.reshape(2, signal.shape[1], lower, second)
    section = jnp.einsum("brnm,abnk->arkm", folded, forward_first[:, :, :lower], precision=precise)
    turned = jnp.stack(
        [
            section[0] * cos_twist + section[1] * sin_twist,
            section[1] * cos_twist - section[0] * sin_twist,
        ]
    )
    return jnp.einsum("brkm,abmj->arkj", turned, forward_second, precision=precise)


def inverse_spectrum(spectrum, tables, first, second, both):
    forward_first, inverse_first, forward_second, inverse_second, cos_twist, sin_twist = tables
    lower = first // 2
    rows = spectrum.shape[1]
    inner = jnp.einsum("brkj,abjm->arkm", spectrum, inverse_second, precision=precise)
    turned = jnp.stack(
        [inner[0] * cos_twist - inner[1] * sin_twist, inner[1] * cos_twist + inner[0] * sin_twist]
    )
    if both:
        signal = jnp.einsum(
            "brkm,abkn->arnm", turned, inverse_first[:, :, :, :lower], precision=precise
        )
        return (signal / (first * second)).reshape(2, rows, lower * second)
    signal = jnp.einsum("brkm,bkn->rnm", turned, inverse_first[0][:, :, :lower], precision=precise)
    return (signal / (first * second)).reshape(rows, lower * second)


def complex_product(left, right):
    return jnp.stack(
        [left[0] * right[0] - left[1] * right[1], left[0] * right[1] + left[1] * right[0]]
    )


def conjugate_product(left, right):
    return jnp.stack(
        [left[0] * right[0] + left[1] * right[1], left[0] * right[1] - left[1] * right[0]]
    )


def mirror(array, seq_dim):
    moved = array
    for bit_index in range(lax.axis_size("seq").bit_length() - 1):
        moved = swapped(moved, "seq", bit_index)
    return jnp.flip(moved, axis=seq_dim)


def to_channels(stacked):
    return lax.all_to_all(stacked, "seq", split_axis=1, concat_axis=2, tiled=True)


def to_tokens(stacked):
    return lax.all_to_all(stacked, "seq", split_axis=2, concat_axis=1, tiled=True)


def body(tokens, w_query, w_value, w_out, long_filter, cotangent):
    floats = jnp.float32
    halves = jnp.bfloat16
    half = w_query.shape[0]
    seq_count = lax.axis_size("seq")
    batch_count = lax.axis_size("batch")
    length = tokens.shape[1] * seq_count
    first, second = split_sizes(length)
    tables = make_tables(first, second)
    scale = (2.0 * batch_count * length) ** (-0.5)
    source = tokens[0]
    front = source[:, :half]
    back = source[:, half:]
    back_strand = mirror(back, 0)[:, ::-1]
    strands = jnp.stack([front, back_strand])
    query = jnp.einsum("stk,kh->sht", strands, w_query, preferred_element_type=floats).astype(
        halves
    )
    value = jnp.einsum("stk,kh->sht", strands, w_value, preferred_element_type=floats).astype(
        halves
    )
    value_sig = to_channels(value).astype(floats)
    value_spec = forward_spectrum(value_sig, tables, first, second)
    taps_spec = forward_spectrum(
        jnp.stack([long_filter, jnp.zeros_like(long_filter)]), tables, first, second
    )
    conv_sig = inverse_spectrum(complex_product(value_spec, taps_spec), tables, first, second, True)
    conv_tok = to_tokens(conv_sig.astype(halves))
    gated = (query.astype(floats) * conv_tok.astype(floats)).astype(halves)
    gated_back = mirror(gated[1], 1)
    out_front = jnp.einsum("ht,hk->tk", gated[0], w_out, preferred_element_type=floats)
    out_back = jnp.einsum("ht,hk->tk", gated_back, w_out, preferred_element_type=floats)
    block_out = jnp.concatenate(
        [front.astype(floats) + out_front, back.astype(floats) + out_back[:, ::-1]], axis=1
    ).astype(halves)[None]
    upstream = cotangent[0]
    up_front = upstream[:, :half]
    up_back = upstream[:, half:]
    grad_back = mirror(up_back, 0)[:, ::-1]
    grad_strands = jnp.stack([up_front, grad_back])
    grad_gated = jnp.einsum(
        "stk,hk->sht", grad_strands, w_out, preferred_element_type=floats
    ).astype(halves)
    grad_query_t = (grad_gated.astype(floats) * conv_tok.astype(floats)).astype(halves)
    grad_conv = (grad_gated.astype(floats) * query.astype(floats)).astype(halves)
    grad_sig = to_channels(grad_conv).astype(floats)
    grad_spec = forward_spectrum(grad_sig, tables, first, second)
    value_grad_sig = inverse_spectrum(
        conjugate_product(taps_spec, grad_spec), tables, first, second, True
    )
    filter_part = (
        inverse_spectrum(conjugate_product(value_spec, grad_spec), tables, first, second, False)
        * scale
    )
    grad_value_t = to_tokens(value_grad_sig.astype(halves))
    front_in = jnp.einsum(
        "ht,kh->tk", grad_query_t[0], w_query, preferred_element_type=floats
    ) + jnp.einsum("ht,kh->tk", grad_value_t[0], w_value, preferred_element_type=floats)
    paired = jnp.stack([grad_query_t[1], grad_value_t[1]])
    paired = mirror(paired, 2)
    back_in = jnp.einsum(
        "ht,kh->tk", paired[0], w_query, preferred_element_type=floats
    ) + jnp.einsum("ht,kh->tk", paired[1], w_value, preferred_element_type=floats)
    grad_tokens = jnp.concatenate(
        [up_front.astype(floats) + front_in, up_back.astype(floats) + back_in[:, ::-1]], axis=1
    ).astype(halves)[None]
    term_query = jnp.einsum("stk,sht->kh", strands, grad_query_t, preferred_element_type=floats)
    term_value = jnp.einsum("stk,sht->kh", strands, grad_value_t, preferred_element_type=floats)
    term_out = jnp.einsum("sht,stk->hk", gated, grad_strands, preferred_element_type=floats)
    share = lax.psum_scatter(
        jnp.concatenate([term_query, term_value, term_out], axis=1) * scale,
        "seq",
        scatter_dimension=0,
        tiled=True,
    )
    share, filter_total = (
        lax.psum(share.astype(jnp.bfloat16), "batch").astype(jnp.float32),
        lax.psum(filter_part.astype(jnp.bfloat16), "batch").astype(jnp.float32),
    )
    return (
        block_out,
        grad_tokens,
        share[:, :half],
        share[:, half : 2 * half],
        share[:, 2 * half :],
        filter_total,
    )

MESH = pl.DeviceIdType.MESH


def angle_parts(length):
    step = 1 << (length.bit_length() - 1) // 2
    angle = np.pi * (np.arange(length) + 0.5)[None] / length
    coarse = np.arange(length // step)[:, None] * step * angle
    fine = np.arange(step)[:, None] * angle
    return (
        np.stack([np.cos(coarse), np.sin(coarse)]).astype(np.float32),
        np.stack([np.cos(fine), np.sin(fine)]).astype(np.float32),
    )


def matmul(left, right):
    return jnp.dot(left, right, preferred_element_type=jnp.float32)


def matmul_t(left, right):
    return lax.dot_general(
        left, right, (((1,), (1,)), ((), ())), preferred_element_type=jnp.float32
    )


def times(x, h, conj):
    size = x.shape[1] // 2
    xr, xs, hr, hs = x[:, :size], x[:, size:], h[:, :size], h[:, size:]
    if conj:
        return xr * hr + xs * hs, xs * hr - xr * hs
    return xr * hr - xs * hs, xr * hs + xs * hr


def fused(
    scale,
    tok_in, wq_in, wv_in, wo_in, taps_in, cot_in, coarse_in, fine_in,
    block_out, grad_out, out_w, out_f,
    tok, wq, wv, wo, taps, cot, coarse, fine, lsem,
    table, strands, ups, strands_t, query, gates, send1, recv1, send2, recv2,
    both_taps, vspec, gspec, hspec, yspec, fspec,
    ssem1, rsem1, lsem1, ssem2, rsem2, lsem2, ssem_t, rsem_t,
    acc, kept, send_a, recv_a, send_b, recv_b, send_c, recv_c,
    kept_z, send_z, recv_z, send_x, recv_x,
    acc_f, kept_f, last_f, send_af, recv_af, send_bf, recv_bf, send_cf, recv_cf,
    ssem_a, rsem_a, ssem_b, rsem_b, ssem_c, rsem_c, ssem_d, rsem_d,
):
    peers, batches = lax.axis_size("seq"), lax.axis_size("batch")
    me, seat = lax.axis_index("seq"), lax.axis_index("batch")
    here, half = tok.shape[0], wq.shape[0]
    f32, b16 = jnp.float32, jnp.bfloat16
    own = half // peers
    length = here * peers
    quarter = own // batches
    mates = peers // 2
    wide = mates * here
    rows = 2 * own
    side, seat_in_side = me // mates, lax.rem(me, mates)
    other = 1 - side
    sign = (2 * side - 1).astype(f32)
    column, level = lax.rem(me, 2), me // 2
    levels = peers // 2
    low, high = lax.rem(seat, 2), seat // 2
    slot = 2 * low + high

    barrier = pltpu.get_barrier_semaphore()
    across = me + 1 - 2 * column
    facing = seat + 2 - 4 * high
    for r in range(1, peers):
        pl.semaphore_signal(
            barrier, inc=1, device_id={"seq": lax.rem(me + r, peers)}, device_id_type=MESH
        )
    for r in range(1, batches):
        pl.semaphore_signal(
            barrier, inc=1, device_id={"batch": lax.rem(seat + r, batches)}, device_id_type=MESH
        )
    pl.semaphore_signal(
        barrier, inc=1, device_id={"seq": across, "batch": facing}, device_id_type=MESH
    )
    loads = {}
    pairs = (
        ("tok", tok_in, tok), ("wv", wv_in, wv), ("taps", taps_in, taps), ("cot", cot_in, cot),
        ("wo", wo_in, wo), ("wq", wq_in, wq), ("coarse", coarse_in, coarse), ("fine", fine_in, fine),
    )
    for index, (name, src, dst) in enumerate(pairs):
        loads[name] = pltpu.make_async_copy(src, dst, lsem.at[index])
        loads[name].start()

    def remote(src, dst, ssem, rsem, **device):
        copy = pltpu.make_async_remote_copy(
            src_ref=src, dst_ref=dst, send_sem=ssem, recv_sem=rsem,
            device_id=device, device_id_type=MESH,
        )
        copy.start()
        return copy

    def local(src, dst, sem):
        copy = pltpu.make_async_copy(src, dst, sem)
        copy.start()
        return copy

    def wait(copies):
        for c in copies:
            c.wait()

    flip = (
        lax.broadcasted_iota(jnp.int32, (half, half), 0)
        + lax.broadcasted_iota(jnp.int32, (half, half), 1)
        == half - 1
    ).astype(f32).astype(b16)

    def stage_rows(index, x):
        turned = x.T
        for bh in range(2):
            for bj in range(mates):
                start = (bh * mates + bj) * own
                send1[index, bj, bh] = turned[start : start + own]

    loads["tok"].wait()
    strands[:here] = tok[:, :half]
    strands[here:] = matmul(tok[:, half:], flip).astype(b16)
    loads["wv"].wait()
    value = matmul(strands[...], wv[...]).astype(b16)
    stage_rows(0, value[:here])
    stage_rows(1, value[here:])
    loads["taps"].wait()
    both_taps[pl.ds(side, 1)] = taps[...].astype(b16).reshape(1, batches, quarter, length)
    pl.semaphore_wait(barrier, peers + batches - 1)

    partner = lax.rem(me + mates, peers)
    tap_copy = remote(
        both_taps.at[side, seat], both_taps.at[side, seat], ssem_t.at[0], rsem_t.at[0], seq=partner
    )

    def out1_cross(d):
        c = 2 * d + (side if d == 0 else other)
        copies = []
        for r in range(mates):
            q = lax.rem(seat_in_side + r, mates)
            copies.append(
                remote(
                    send1.at[c, q], recv1.at[c, me], ssem1.at[d, mates + r], rsem1.at[d, mates + r],
                    seq=other * mates + q,
                )
            )
        return copies

    def out1_own(d):
        pair = pl.ds(2 * d, 2)
        copies = []
        for r in range(1, mates):
            q = lax.rem(seat_in_side + r, mates)
            copies.append(
                remote(
                    send1.at[pair, q], recv1.at[pair, me], ssem1.at[d, r], rsem1.at[d, r],
                    seq=side * mates + q,
                )
            )
        copies.append(local(send1.at[pair, seat_in_side], recv1.at[pair, me], lsem1.at[d]))
        return copies

    def out2(k, c):
        copies = []
        for r in range(1, mates):
            q = lax.rem(seat_in_side + r, mates)
            copies.append(
                remote(
                    send2.at[c, q], recv2.at[c, seat_in_side], ssem2.at[k, r], rsem2.at[k, r],
                    seq=side * mates + q,
                )
            )
        copies.append(local(send2.at[c, seat_in_side], recv2.at[c, seat_in_side], lsem2.at[k]))
        return copies

    own_v = out1_own(0)
    cross_v = out1_cross(0)

    for name in ("cot", "wo", "wq"):
        loads[name].wait()
    ups[:here] = cot[:, :half]
    ups[here:] = matmul(cot[:, half:], flip).astype(b16)
    query[...] = matmul(strands[...], wq[...]).astype(b16)
    gates[...] = matmul_t(ups[...], wo[...]).astype(b16)
    grad_conv = (gates[...].astype(f32) * query[...].astype(f32)).astype(b16)
    stage_rows(2, grad_conv[:here])
    stage_rows(3, grad_conv[here:])
    own_g = out1_own(1)
    cross_g = out1_cross(1)

    for name in ("coarse", "fine"):
        loads[name].wait()
    count, step = coarse.shape[1], fine.shape[1]

    @pl.loop(0, count)
    def _(a):
        ca, sa = coarse[0, pl.ds(a, 1), :], coarse[1, pl.ds(a, 1), :]
        at = pl.ds(pl.multiple_of(a * step, step), step)
        table[at, :length] = (ca * fine[0] - sa * fine[1]).astype(b16)
        table[at, length:] = (sa * fine[0] + ca * fine[1]).astype(b16)

    tap_copy.wait()
    tap_copies = [
        remote(
            both_taps.at[other, seat], both_taps.at[other, seat], ssem_t.at[r], rsem_t.at[r],
            batch=lax.rem(seat + r, batches),
        )
        for r in range(1, batches)
    ]
    strands_t[...] = strands[...].T

    def rows_at(i):
        return pl.ds(pl.multiple_of(i * rows, rows), rows)

    def table_of(which):
        return table[pl.ds(pl.multiple_of(which * wide, wide), wide), :]

    def signal(c, which):
        return jnp.concatenate(
            [recv1[c, which * mates + i].reshape(rows, here) for i in range(mates)], axis=1
        )

    def own_signals(d):
        return jnp.concatenate([signal(2 * d, side), signal(2 * d + 1, side)], axis=0)

    def returned(k, c, spec, conj):
        r, s = times(spec, hspec[...], conj)
        yspec[k, :, :length] = r.astype(b16)
        yspec[k, :, length:] = s.astype(b16)
        back = (matmul_t(yspec[k], table_of(side)) * (1.0 / length)).astype(b16)
        for q in range(mates):
            send2[pl.ds(c, 1), q] = back[:, q * here : (q + 1) * here].reshape(1, 2, own, here)
        return out2(k, c)

    def part_of(bit, size):
        return pl.ds(pl.multiple_of(bit * size, size), size)

    def weight(m, product):
        acc[m] = (product * scale).reshape(levels, 2, own, half)

    def stage_a(m):
        send_a[m] = acc[m, :, :, part_of(1 - low, 2 * quarter), :].astype(b16)
        return remote(
            send_a.at[m], recv_a.at[m], ssem_a.at[m], rsem_a.at[m], batch=2 * high + 1 - low
        )

    def stage_b(m, copy):
        copy.wait()

        def pick(x, y):
            at = pl.ds(pl.multiple_of((2 * low + y) * quarter, quarter), quarter)
            mine = acc[m, :, pl.ds(x, 1), at, :]
            theirs = recv_a[m, :, pl.ds(x, 1), part_of(y, quarter), :].astype(f32)
            return (mine + theirs).reshape(levels, quarter, half)

        copies = []
        for index, (dx, dy) in enumerate(((1, 1), (1, 0), (0, 1))):
            x = 1 - column if dx else column
            y = 1 - high if dy else high
            send_b[m, index] = pick(x, y).astype(b16)
            copies.append(
                remote(
                    send_b.at[m, index], recv_b.at[m, index], ssem_b.at[m, index],
                    rsem_b.at[m, index], seq=across if dx else me, batch=facing if dy else seat,
                )
            )
        kept[m] = pick(column, high)
        return copies

    def stage_c(m, copies):
        wait(copies)
        send_c[m] = (kept[m] + jnp.sum(recv_b[m].astype(f32), axis=0)).astype(b16)
        copies = []
        for r in range(1, levels):
            z = lax.rem(level + r, levels)
            copies.append(
                remote(
                    send_c.at[m, z], recv_c.at[m, level], ssem_c.at[m, r], rsem_c.at[m, r],
                    seq=2 * z + column,
                )
            )
        recv_c[m, level] = send_c[m, level]
        return copies

    def share(m, whole):
        return [
            remote(
                whole.at[slot], whole.at[slot], ssem_d.at[m, r], rsem_d.at[m, r],
                batch=lax.rem(seat + r, batches),
            )
            for r in range(1, batches)
        ]

    def stage_bz(m, copy):
        copy.wait()

        def pick(z):
            mine = acc[m, pl.ds(z, 1), :, part_of(low, 2 * quarter), :]
            return (mine + recv_a[m, pl.ds(z, 1)].astype(f32)).reshape(2, 2 * quarter, half)

        copies = []
        for r in range(1, levels):
            z = lax.rem(level + r, levels)
            send_z[r - 1] = pick(z).astype(b16)
            copies.append(
                remote(
                    send_z.at[r - 1], recv_z.at[r - 1], ssem_b.at[m, r - 1], rsem_b.at[m, r - 1],
                    seq=2 * z + column,
                )
            )
        kept_z[...] = pick(level)
        return copies

    def stage_cz(m, copies):
        wait(copies)
        kept_z[...] = kept_z[...] + jnp.sum(recv_z[...].astype(f32), axis=0)
        copies = []
        for index, (dx, dy) in enumerate(((1, 1), (1, 0), (0, 1))):
            x = 1 - column if dx else column
            y = 1 - high if dy else high
            send_x[index] = kept_z[x, part_of(y, quarter), :].astype(b16)
            copies.append(
                remote(
                    send_x.at[index], recv_x.at[index], ssem_c.at[m, index], rsem_c.at[m, index],
                    seq=across if dx else me, batch=facing if dy else seat,
                )
            )
        return copies

    def stage_dz(m, copies):
        wait(copies)
        mine = kept_z[column, part_of(high, quarter), :]
        out_w[m, slot] = (mine + jnp.sum(recv_x[...].astype(f32), axis=0)).astype(b16)
        return share(m, out_w.at[m])

    def stage_d(m, copies):
        wait(copies)
        out_w[m, slot] = jnp.sum(recv_c[m].astype(f32), axis=0).astype(b16)
        return share(m, out_w.at[m])

    def rejoin(c):
        return jnp.concatenate(
            [recv2[c, bj, bh] for bh in range(2) for bj in range(mates)], axis=0
        ).T

    wait(own_v)
    vspec[...] = matmul(own_signals(0), table_of(side))
    wait(tap_copies)
    hspec[...] = matmul(both_taps[...].reshape(rows, length), table[...])
    hspec[:, length:] = hspec[:, length:] * sign
    self_v = returned(0, side, vspec[rows_at(side), :], True)
    wait(cross_v)
    vspec[rows_at(other), :] = vspec[rows_at(other), :] + matmul(
        signal(other, other), table_of(other)
    )
    full_v = returned(1, other, vspec[rows_at(other), :], False)
    wait(own_g)
    gspec[...] = matmul(own_signals(1), table_of(side))
    self_g = returned(2, 2 + other, gspec[rows_at(other), :], True)
    r0, s0 = times(gspec[rows_at(other), :], vspec[rows_at(other), :], True)
    r1, s1 = times(gspec[rows_at(side), :], vspec[rows_at(side), :], True)
    fspec[:, :length] = (r0 + r1).astype(b16)
    fspec[:, length:] = ((s0 - s1) * sign).astype(b16)
    acc_f[...] = (matmul_t(fspec[...], table[...]) * (scale / length)).reshape(2, own, length)
    send_af[...] = acc_f[:, part_of(1 - low, 2 * quarter), :].astype(b16)
    af = remote(send_af, recv_af, ssem_a.at[3], rsem_a.at[3], batch=2 * high + 1 - low)
    af.wait()
    kept_f[...] = acc_f[:, part_of(low, 2 * quarter), :] + recv_af[...].astype(f32)
    send_bf[...] = kept_f[:, part_of(1 - high, quarter), :].astype(b16)
    bf = remote(send_bf, recv_bf, ssem_b.at[3, 0], rsem_b.at[3, 0], batch=facing)
    wait(cross_g)
    gspec[rows_at(side), :] = gspec[rows_at(side), :] + matmul(
        signal(2 + side, other), table_of(other)
    )
    full_g = returned(3, 2 + side, gspec[rows_at(side), :], False)
    wait(self_v)
    wait(full_v)
    conv = jnp.concatenate([rejoin(0), rejoin(1)], axis=0).astype(f32)
    grad_query = (gates[...].astype(f32) * conv).astype(b16)
    weight(0, matmul(strands_t[...], grad_query))
    a0 = stage_a(0)
    gated = (query[...].astype(f32) * conv).astype(b16)
    weight(1, matmul(gated.T, ups[...]))
    a1 = stage_a(1)
    b0 = stage_b(0, a0)
    b1 = stage_bz(1, a1)
    wait(self_g)
    wait(full_g)
    value_0, value_1 = rejoin(2), rejoin(3)
    grad_value = jnp.concatenate([value_0, value_1], axis=0)
    weight(2, matmul(strands_t[...], grad_value))
    a2 = stage_a(2)
    total = strands[...].astype(f32) + matmul(gated, wo[...])
    block_out[:, :half] = total[:here].astype(b16)
    last = total[here:].astype(b16)
    b2 = stage_b(2, a2)
    bf.wait()
    last_f[...] = kept_f[:, part_of(high, quarter), :] + recv_bf[...].astype(f32)
    send_cf[...] = last_f[other].astype(b16)
    cf = remote(send_cf, recv_cf, ssem_c.at[3, 0], rsem_c.at[3, 0], seq=partner)
    block_out[:, half:] = matmul(last, flip).astype(b16)
    c0 = stage_c(0, b0)
    c1 = stage_cz(1, b1)
    total = ups[...].astype(f32) + matmul_t(grad_query, wq[...]) + matmul_t(grad_value, wv[...])
    grad_out[:, :half] = total[:here].astype(b16)
    grad_out[:, half:] = matmul(total[here:].astype(b16), flip).astype(b16)
    d0 = stage_d(0, c0)
    c2 = stage_c(2, b2)
    cf.wait()
    out_f[slot] = (last_f[side] + recv_cf[...].astype(f32)).astype(b16)
    df = share(3, out_f)
    d1 = stage_dz(1, c1)
    wait(d0)
    d2 = stage_d(2, c2)
    wait(df)
    wait(d1)
    wait(d2)


def emit(
    block, grad_tok, weights, filters,
    block_out, grad_out, out_q, out_v, out_o, out_f,
    wide_w, wide_f, sem,
):
    copies = []

    def leave(src, dst):
        copy = pltpu.make_async_copy(src, dst, sem.at[len(copies)])
        copy.start()
        copies.append(copy)

    leave(block, block_out)
    leave(grad_tok, grad_out)
    wide_f[...] = filters[...].reshape(wide_f.shape).astype(wide_f.dtype)
    leave(wide_f, out_f)
    for m, dst in enumerate((out_q, out_o, out_v)):
        wide_w[m] = weights[m].reshape(dst.shape).astype(wide_w.dtype)
        leave(wide_w.at[m], dst)
    for copy in copies:
        copy.wait()


def short_body(tokens, w_query, w_value, w_out, long_filter, cotangent):
    f32, b16 = jnp.float32, jnp.bfloat16
    half = w_query.shape[0]
    peers = lax.axis_size("seq")
    here = tokens.shape[1]
    length = here * peers
    own = half // peers
    scale = (2.0 * lax.axis_size("batch") * length) ** (-0.5)
    coarse, fine = angle_parts(length)
    dma = pltpu.SemaphoreType.DMA
    batches = lax.axis_size("batch")
    quarter = own // batches
    mates = levels = peers // 2
    vmem = pltpu.VMEM
    arguments = (tokens[0], w_query, w_value, w_out, long_filter, cotangent[0], coarse, fine)
    block, grad_tok, weights, filters = pl.pallas_call(
        functools.partial(fused, scale),
        out_shape=(
            vmem((here, 2 * half), b16),
            vmem((here, 2 * half), b16),
            vmem((3, batches, quarter, half), b16),
            vmem((batches, quarter, length), b16),
        ),
        in_specs=[pl.BlockSpec(memory_space=pltpu.HBM)] * 8,
        out_specs=(pl.BlockSpec(memory_space=pltpu.VMEM),) * 4,
        scratch_shapes=[
            *(vmem(a.shape, a.dtype) for a in arguments),
            dma((8,)),
            vmem((length, 2 * length), b16),
            vmem((2 * here, half), b16),
            vmem((2 * here, half), b16),
            vmem((half, 2 * here), b16),
            vmem((2 * here, half), b16),
            vmem((2 * here, half), b16),
            vmem((4, mates, 2, own, here), b16),
            vmem((4, peers, 2, own, here), b16),
            vmem((4, mates, 2, own, here), b16),
            vmem((4, mates, 2, own, here), b16),
            vmem((2, batches, quarter, length), b16),
            vmem((4 * own, 2 * length), f32),
            vmem((4 * own, 2 * length), f32),
            vmem((2 * own, 2 * length), f32),
            vmem((4, 2 * own, 2 * length), b16),
            vmem((2 * own, 2 * length), b16),
            dma((2, peers)),
            dma((2, peers)),
            dma((2,)),
            dma((4, mates)),
            dma((4, mates)),
            dma((4,)),
            dma((batches,)),
            dma((batches,)),
            vmem((3, levels, 2, own, half), f32),
            vmem((3, levels, quarter, half), f32),
            vmem((3, levels, 2, 2 * quarter, half), b16),
            vmem((3, levels, 2, 2 * quarter, half), b16),
            vmem((3, 3, levels, quarter, half), b16),
            vmem((3, 3, levels, quarter, half), b16),
            vmem((3, levels, quarter, half), b16),
            vmem((3, levels, quarter, half), b16),
            vmem((2, 2 * quarter, half), f32),
            vmem((3, 2, 2 * quarter, half), b16),
            vmem((3, 2, 2 * quarter, half), b16),
            vmem((3, quarter, half), b16),
            vmem((3, quarter, half), b16),
            vmem((2, own, length), f32),
            vmem((2, 2 * quarter, length), f32),
            vmem((2, quarter, length), f32),
            vmem((2, 2 * quarter, length), b16),
            vmem((2, 2 * quarter, length), b16),
            vmem((2, quarter, length), b16),
            vmem((2, quarter, length), b16),
            vmem((quarter, length), b16),
            vmem((quarter, length), b16),
            dma((4,)),
            dma((4,)),
            dma((4, 3)),
            dma((4, 3)),
            dma((4, levels)),
            dma((4, levels)),
            dma((4, batches)),
            dma((4, batches)),
        ],
        compiler_params=pltpu.CompilerParams(
            collective_id=0, has_side_effects=True, vmem_limit_bytes=65900000
        ),
    )(*arguments)
    block, grad_tok, *sums = pl.pallas_call(
        emit,
        out_shape=(
            jax.ShapeDtypeStruct((here, 2 * half), b16),
            jax.ShapeDtypeStruct((here, 2 * half), b16),
            jax.ShapeDtypeStruct((own, half), f32),
            jax.ShapeDtypeStruct((own, half), f32),
            jax.ShapeDtypeStruct((own, half), f32),
            jax.ShapeDtypeStruct((own, length), f32),
        ),
        in_specs=[pl.BlockSpec(memory_space=pltpu.VMEM)] * 4,
        out_specs=(pl.BlockSpec(memory_space=pltpu.HBM),) * 6,
        scratch_shapes=[vmem((3, own, half), f32), vmem((own, length), f32), dma((6,))],
        compiler_params=pltpu.CompilerParams(vmem_limit_bytes=8000000),
    )(block, grad_tok, weights, filters)
    return (block[None], grad_tok[None], *sums)


def fits(tokens, half):
    peers, batches = lax.axis_size("seq"), lax.axis_size("batch")
    small = (tokens.shape[1] * peers) ** 2 * 4 <= 8 << 20
    square = peers == 8 and batches == 4 and tokens.shape[1] % 128 == 0
    return small and square and half % (16 * batches * peers) == 0


def choose(tokens, *rest):
    short = fits(tokens, rest[0].shape[0])
    return (short_body if short else body)(tokens, *rest)


def solution(mesh):
    in_specs = (P("batch", "seq", None), P(), P(), P(), P("seq", None), P("batch", "seq", None))
    out_specs = (
        P("batch", "seq", None),
        P("batch", "seq", None),
        P("seq", None),
        P("seq", None),
        P("seq", None),
        P("seq", None),
    )
    return jax.shard_map(choose, mesh=mesh, in_specs=in_specs, out_specs=out_specs, check_vma=False)
```

```python
import functools
import math

import jax
import jax.numpy as jnp
import numpy as np
from jax import lax
from jax.experimental import pallas as pl
from jax.experimental.pallas import tpu as pltpu
from jax.sharding import PartitionSpec as P

precise = lax.Precision.HIGH


def swapped(x, axis, stride):
    return lax.ppermute(x, axis, [(i, i ^ 1 << stride) for i in range(lax.axis_size(axis))])


def angle_tables(count_rows, count_cols, period):
    left = lax.broadcasted_iota(jnp.int32, (count_rows, count_cols), 0)
    right = lax.broadcasted_iota(jnp.int32, (count_rows, count_cols), 1)
    turns = left * right % period
    angle = turns.astype(jnp.float32) * (2.0 * math.pi / period)
    return (jnp.cos(angle), jnp.sin(angle))


def rotation(cosines, sines, direction):
    upper = jnp.stack([cosines, direction * sines])
    lower_row = jnp.stack([-direction * sines, cosines])
    return jnp.stack([upper, lower_row])


def split_sizes(length):
    period = 2 * length
    first = 1 << (period.bit_length() - 1 + 1) // 2
    return (first, period // first)


def make_tables(first, second):
    cos_first, sin_first = angle_tables(first, first, first)
    cos_twist, sin_twist = angle_tables(first, second, first * second)
    cos_second, sin_second = angle_tables(second, second, second)
    forward_first = rotation(cos_first, sin_first, 1.0)
    inverse_first = rotation(cos_first, sin_first, -1.0)
    forward_second = rotation(cos_second, sin_second, 1.0)
    inverse_second = rotation(cos_second, sin_second, -1.0)
    return (forward_first, inverse_first, forward_second, inverse_second, cos_twist, sin_twist)


def forward_spectrum(signal, tables, first, second):
    forward_first, inverse_first, forward_second, inverse_second, cos_twist, sin_twist = tables
    lower = first // 2
    folded = signal.reshape(2, signal.shape[1], lower, second)
    section = jnp.einsum("brnm,abnk->arkm", folded, forward_first[:, :, :lower], precision=precise)
    turned = jnp.stack(
        [
            section[0] * cos_twist + section[1] * sin_twist,
            section[1] * cos_twist - section[0] * sin_twist,
        ]
    )
    return jnp.einsum("brkm,abmj->arkj", turned, forward_second, precision=precise)


def inverse_spectrum(spectrum, tables, first, second, both):
    forward_first, inverse_first, forward_second, inverse_second, cos_twist, sin_twist = tables
    lower = first // 2
    rows = spectrum.shape[1]
    inner = jnp.einsum("brkj,abjm->arkm", spectrum, inverse_second, precision=precise)
    turned = jnp.stack(
        [inner[0] * cos_twist - inner[1] * sin_twist, inner[1] * cos_twist + inner[0] * sin_twist]
    )
    if both:
        signal = jnp.einsum(
            "brkm,abkn->arnm", turned, inverse_first[:, :, :, :lower], precision=precise
        )
        return (signal / (first * second)).reshape(2, rows, lower * second)
    signal = jnp.einsum("brkm,bkn->rnm", turned, inverse_first[0][:, :, :lower], precision=precise)
    return (signal / (first * second)).reshape(rows, lower * second)


def complex_product(left, right):
    return jnp.stack(
        [left[0] * right[0] - left[1] * right[1], left[0] * right[1] + left[1] * right[0]]
    )


def conjugate_product(left, right):
    return jnp.stack(
        [left[0] * right[0] + left[1] * right[1], left[0] * right[1] - left[1] * right[0]]
    )


def mirror(array, seq_dim):
    moved = array
    for bit_index in range(lax.axis_size("seq").bit_length() - 1):
        moved = swapped(moved, "seq", bit_index)
    return jnp.flip(moved, axis=seq_dim)


def to_channels(stacked):
    return lax.all_to_all(stacked, "seq", split_axis=1, concat_axis=2, tiled=True)


def to_tokens(stacked):
    return lax.all_to_all(stacked, "seq", split_axis=2, concat_axis=1, tiled=True)


def body(tokens, w_query, w_value, w_out, long_filter, cotangent):
    floats = jnp.float32
    halves = jnp.bfloat16
    half = w_query.shape[0]
    seq_count = lax.axis_size("seq")
    batch_count = lax.axis_size("batch")
    length = tokens.shape[1] * seq_count
    first, second = split_sizes(length)
    tables = make_tables(first, second)
    scale = (2.0 * batch_count * length) ** (-0.5)
    source = tokens[0]
    front = source[:, :half]
    back = source[:, half:]
    back_strand = mirror(back, 0)[:, ::-1]
    strands = jnp.stack([front, back_strand])
    query = jnp.einsum("stk,kh->sht", strands, w_query, preferred_element_type=floats).astype(
        halves
    )
    value = jnp.einsum("stk,kh->sht", strands, w_value, preferred_element_type=floats).astype(
        halves
    )
    value_sig = to_channels(value).astype(floats)
    value_spec = forward_spectrum(value_sig, tables, first, second)
    taps_spec = forward_spectrum(
        jnp.stack([long_filter, jnp.zeros_like(long_filter)]), tables, first, second
    )
    conv_sig = inverse_spectrum(complex_product(value_spec, taps_spec), tables, first, second, True)
    conv_tok = to_tokens(conv_sig.astype(halves))
    gated = (query.astype(floats) * conv_tok.astype(floats)).astype(halves)
    gated_back = mirror(gated[1], 1)
    out_front = jnp.einsum("ht,hk->tk", gated[0], w_out, preferred_element_type=floats)
    out_back = jnp.einsum("ht,hk->tk", gated_back, w_out, preferred_element_type=floats)
    block_out = jnp.concatenate(
        [front.astype(floats) + out_front, back.astype(floats) + out_back[:, ::-1]], axis=1
    ).astype(halves)[None]
    upstream = cotangent[0]
    up_front = upstream[:, :half]
    up_back = upstream[:, half:]
    grad_back = mirror(up_back, 0)[:, ::-1]
    grad_strands = jnp.stack([up_front, grad_back])
    grad_gated = jnp.einsum(
        "stk,hk->sht", grad_strands, w_out, preferred_element_type=floats
    ).astype(halves)
    grad_query_t = (grad_gated.astype(floats) * conv_tok.astype(floats)).astype(halves)
    grad_conv = (grad_gated.astype(floats) * query.astype(floats)).astype(halves)
    grad_sig = to_channels(grad_conv).astype(floats)
    grad_spec = forward_spectrum(grad_sig, tables, first, second)
    value_grad_sig = inverse_spectrum(
        conjugate_product(taps_spec, grad_spec), tables, first, second, True
    )
    filter_part = (
        inverse_spectrum(conjugate_product(value_spec, grad_spec), tables, first, second, False)
        * scale
    )
    grad_value_t = to_tokens(value_grad_sig.astype(halves))
    front_in = jnp.einsum(
        "ht,kh->tk", grad_query_t[0], w_query, preferred_element_type=floats
    ) + jnp.einsum("ht,kh->tk", grad_value_t[0], w_value, preferred_element_type=floats)
    paired = jnp.stack([grad_query_t[1], grad_value_t[1]])
    paired = mirror(paired, 2)
    back_in = jnp.einsum(
        "ht,kh->tk", paired[0], w_query, preferred_element_type=floats
    ) + jnp.einsum("ht,kh->tk", paired[1], w_value, preferred_element_type=floats)
    grad_tokens = jnp.concatenate(
        [up_front.astype(floats) + front_in, up_back.astype(floats) + back_in[:, ::-1]], axis=1
    ).astype(halves)[None]
    term_query = jnp.einsum("stk,sht->kh", strands, grad_query_t, preferred_element_type=floats)
    term_value = jnp.einsum("stk,sht->kh", strands, grad_value_t, preferred_element_type=floats)
    term_out = jnp.einsum("sht,stk->hk", gated, grad_strands, preferred_element_type=floats)
    share = lax.psum_scatter(
        jnp.concatenate([term_query, term_value, term_out], axis=1) * scale,
        "seq",
        scatter_dimension=0,
        tiled=True,
    )
    share, filter_total = (
        lax.psum(share.astype(jnp.bfloat16), "batch").astype(jnp.float32),
        lax.psum(filter_part.astype(jnp.bfloat16), "batch").astype(jnp.float32),
    )
    return (
        block_out,
        grad_tokens,
        share[:, :half],
        share[:, half : 2 * half],
        share[:, 2 * half :],
        filter_total,
    )

MESH = pl.DeviceIdType.MESH


def angle_parts(length):
    step = 1 << (length.bit_length() - 1) // 2
    angle = np.pi * (np.arange(length) + 0.5)[None] / length
    coarse = np.arange(length // step)[:, None] * step * angle
    fine = np.arange(step)[:, None] * angle
    return (
        np.stack([np.cos(coarse), np.sin(coarse)]).astype(np.float32),
        np.stack([np.cos(fine), np.sin(fine)]).astype(np.float32),
    )


def matmul(left, right):
    return jnp.dot(left, right, preferred_element_type=jnp.float32)


def matmul_t(left, right):
    return lax.dot_general(
        left, right, (((1,), (1,)), ((), ())), preferred_element_type=jnp.float32
    )


def times(x, h, conj):
    size = x.shape[1] // 2
    xr, xs, hr, hs = x[:, :size], x[:, size:], h[:, :size], h[:, size:]
    if conj:
        return xr * hr + xs * hs, xs * hr - xr * hs
    return xr * hr - xs * hs, xr * hs + xs * hr


def fused(
    scale,
    tok_in, wq_in, wv_in, wo_in, taps_in, cot_in, coarse_in, fine_in,
    block_out, grad_out, out_w, out_f,
    tok, wq, wv, wo, taps, cot, coarse, fine, lsem,
    table, strands, ups, strands_t, query, gates, send1, recv1, send2, recv2,
    both_taps, vspec, gspec, hspec, yspec, fspec,
    ssem1, rsem1, lsem1, ssem2, rsem2, lsem2, ssem_t, rsem_t,
    acc, kept, send_a, recv_a, send_b, recv_b, send_c, recv_c,
    kept_z, send_z, recv_z, send_x, recv_x,
    acc_f, kept_f, last_f, send_af, recv_af, send_bf, recv_bf, send_cf, recv_cf,
    ssem_a, rsem_a, ssem_b, rsem_b, ssem_c, rsem_c, ssem_d, rsem_d,
):
    peers, batches = lax.axis_size("seq"), lax.axis_size("batch")
    me, seat = lax.axis_index("seq"), lax.axis_index("batch")
    here, half = tok.shape[0], wq.shape[0]
    f32, b16 = jnp.float32, jnp.bfloat16
    own = half // peers
    length = here * peers
    quarter = own // batches
    mates = peers // 2
    wide = mates * here
    rows = 2 * own
    side, seat_in_side = me // mates, lax.rem(me, mates)
    other = 1 - side
    sign = (2 * side - 1).astype(f32)
    column, level = lax.rem(me, 2), me // 2
    levels = peers // 2
    low, high = lax.rem(seat, 2), seat // 2
    slot = 2 * low + high

    barrier = pltpu.get_barrier_semaphore()
    across = me + 1 - 2 * column
    facing = seat + 2 - 4 * high
    for r in range(1, peers):
        pl.semaphore_signal(
            barrier, inc=1, device_id={"seq": lax.rem(me + r, peers)}, device_id_type=MESH
        )
    for r in range(1, batches):
        pl.semaphore_signal(
            barrier, inc=1, device_id={"batch": lax.rem(seat + r, batches)}, device_id_type=MESH
        )
    pl.semaphore_signal(
        barrier, inc=1, device_id={"seq": across, "batch": facing}, device_id_type=MESH
    )
    loads = {}
    pairs = (
        ("tok", tok_in, tok), ("wv", wv_in, wv), ("taps", taps_in, taps), ("cot", cot_in, cot),
        ("wo", wo_in, wo), ("wq", wq_in, wq), ("coarse", coarse_in, coarse), ("fine", fine_in, fine),
    )
    for index, (name, src, dst) in enumerate(pairs):
        loads[name] = pltpu.make_async_copy(src, dst, lsem.at[index])
        loads[name].start()

    def remote(src, dst, ssem, rsem, **device):
        copy = pltpu.make_async_remote_copy(
            src_ref=src, dst_ref=dst, send_sem=ssem, recv_sem=rsem,
            device_id=device, device_id_type=MESH,
        )
        copy.start()
        return copy

    def local(src, dst, sem):
        copy = pltpu.make_async_copy(src, dst, sem)
        copy.start()
        return copy

    def wait(copies):
        for c in copies:
            c.wait()

    flip = (
        lax.broadcasted_iota(jnp.int32, (half, half), 0)
        + lax.broadcasted_iota(jnp.int32, (half, half), 1)
        == half - 1
    ).astype(f32).astype(b16)

    def stage_rows(index, x):
        turned = x.T
        for bh in range(2):
            for bj in range(mates):
                start = (bh * mates + bj) * own
                send1[index, bj, bh] = turned[start : start + own]

    loads["tok"].wait()
    strands[:here] = tok[:, :half]
    strands[here:] = matmul(tok[:, half:], flip).astype(b16)
    loads["wv"].wait()
    value = matmul(strands[...], wv[...]).astype(b16)
    stage_rows(0, value[:here])
    stage_rows(1, value[here:])
    loads["taps"].wait()
    both_taps[pl.ds(side, 1)] = taps[...].astype(b16).reshape(1, batches, quarter, length)
    pl.semaphore_wait(barrier, peers + batches - 1)

    partner = lax.rem(me + mates, peers)
    tap_copy = remote(
        both_taps.at[side, seat], both_taps.at[side, seat], ssem_t.at[0], rsem_t.at[0], seq=partner
    )

    def out1_cross(d):
        c = 2 * d + (side if d == 0 else other)
        copies = []
        for r in range(mates):
            q = lax.rem(seat_in_side + r, mates)
            copies.append(
                remote(
                    send1.at[c, q], recv1.at[c, me], ssem1.at[d, mates + r], rsem1.at[d, mates + r],
                    seq=other * mates + q,
                )
            )
        return copies

    def out1_own(d):
        pair = pl.ds(2 * d, 2)
        copies = []
        for r in range(1, mates):
            q = lax.rem(seat_in_side + r, mates)
            copies.append(
                remote(
                    send1.at[pair, q], recv1.at[pair, me], ssem1.at[d, r], rsem1.at[d, r],
                    seq=side * mates + q,
                )
            )
        copies.append(local(send1.at[pair, seat_in_side], recv1.at[pair, me], lsem1.at[d]))
        return copies

    def out2(k, c):
        copies = []
        for r in range(1, mates):
            q = lax.rem(seat_in_side + r, mates)
            copies.append(
                remote(
                    send2.at[c, q], recv2.at[c, seat_in_side], ssem2.at[k, r], rsem2.at[k, r],
                    seq=side * mates + q,
                )
            )
        copies.append(local(send2.at[c, seat_in_side], recv2.at[c, seat_in_side], lsem2.at[k]))
        return copies

    own_v = out1_own(0)
    cross_v = out1_cross(0)

    for name in ("cot", "wo", "wq"):
        loads[name].wait()
    ups[:here] = cot[:, :half]
    ups[here:] = matmul(cot[:, half:], flip).astype(b16)
    query[...] = matmul(strands[...], wq[...]).astype(b16)
    gates[...] = matmul_t(ups[...], wo[...]).astype(b16)
    grad_conv = (gates[...].astype(f32) * query[...].astype(f32)).astype(b16)
    stage_rows(2, grad_conv[:here])
    stage_rows(3, grad_conv[here:])
    own_g = out1_own(1)
    cross_g = out1_cross(1)

    for name in ("coarse", "fine"):
        loads[name].wait()
    count, step = coarse.shape[1], fine.shape[1]

    @pl.loop(0, count)
    def _(a):
        ca, sa = coarse[0, pl.ds(a, 1), :], coarse[1, pl.ds(a, 1), :]
        at = pl.ds(pl.multiple_of(a * step, step), step)
        table[at, :length] = (ca * fine[0] - sa * fine[1]).astype(b16)
        table[at, length:] = (sa * fine[0] + ca * fine[1]).astype(b16)

    tap_copy.wait()
    tap_copies = [
        remote(
            both_taps.at[other, seat], both_taps.at[other, seat], ssem_t.at[r], rsem_t.at[r],
            batch=lax.rem(seat + r, batches),
        )
        for r in range(1, batches)
    ]
    strands_t[...] = strands[...].T

    def rows_at(i):
        return pl.ds(pl.multiple_of(i * rows, rows), rows)

    def table_of(which):
        return table[pl.ds(pl.multiple_of(which * wide, wide), wide), :]

    def signal(c, which):
        return jnp.concatenate(
            [recv1[c, which * mates + i].reshape(rows, here) for i in range(mates)], axis=1
        )

    def own_signals(d):
        return jnp.concatenate([signal(2 * d, side), signal(2 * d + 1, side)], axis=0)

    def returned(k, c, spec, conj):
        r, s = times(spec, hspec[...], conj)
        yspec[k, :, :length] = r.astype(b16)
        yspec[k, :, length:] = s.astype(b16)
        back = (matmul_t(yspec[k], table_of(side)) * (1.0 / length)).astype(b16)
        for q in range(mates):
            send2[pl.ds(c, 1), q] = back[:, q * here : (q + 1) * here].reshape(1, 2, own, here)
        return out2(k, c)

    def part_of(bit, size):
        return pl.ds(pl.multiple_of(bit * size, size), size)

    def weight(m, product):
        acc[m] = (product * scale).reshape(levels, 2, own, half)

    def stage_a(m):
        send_a[m] = acc[m, :, :, part_of(1 - low, 2 * quarter), :].astype(b16)
        return remote(
            send_a.at[m], recv_a.at[m], ssem_a.at[m], rsem_a.at[m], batch=2 * high + 1 - low
        )

    def stage_b(m, copy):
        copy.wait()

        def pick(x, y):
            at = pl.ds(pl.multiple_of((2 * low + y) * quarter, quarter), quarter)
            mine = acc[m, :, pl.ds(x, 1), at, :]
            theirs = recv_a[m, :, pl.ds(x, 1), part_of(y, quarter), :].astype(f32)
            return (mine + theirs).reshape(levels, quarter, half)

        copies = []
        for index, (dx, dy) in enumerate(((1, 1), (1, 0), (0, 1))):
            x = 1 - column if dx else column
            y = 1 - high if dy else high
            send_b[m, index] = pick(x, y).astype(b16)
            copies.append(
                remote(
                    send_b.at[m, index], recv_b.at[m, index], ssem_b.at[m, index],
                    rsem_b.at[m, index], seq=across if dx else me, batch=facing if dy else seat,
                )
            )
        kept[m] = pick(column, high)
        return copies

    def stage_c(m, copies):
        wait(copies)
        send_c[m] = (kept[m] + jnp.sum(recv_b[m].astype(f32), axis=0)).astype(b16)
        copies = []
        for r in range(1, levels):
            z = lax.rem(level + r, levels)
            copies.append(
                remote(
                    send_c.at[m, z], recv_c.at[m, level], ssem_c.at[m, r], rsem_c.at[m, r],
                    seq=2 * z + column,
                )
            )
        recv_c[m, level] = send_c[m, level]
        return copies

    def share(m, whole):
        return [
            remote(
                whole.at[slot], whole.at[slot], ssem_d.at[m, r], rsem_d.at[m, r],
                batch=lax.rem(seat + r, batches),
            )
            for r in range(1, batches)
        ]

    def stage_bz(m, copy):
        copy.wait()

        def pick(z):
            mine = acc[m, pl.ds(z, 1), :, part_of(low, 2 * quarter), :]
            return (mine + recv_a[m, pl.ds(z, 1)].astype(f32)).reshape(2, 2 * quarter, half)

        copies = []
        for r in range(1, levels):
            z = lax.rem(level + r, levels)
            send_z[r - 1] = pick(z).astype(b16)
            copies.append(
                remote(
                    send_z.at[r - 1], recv_z.at[r - 1], ssem_b.at[m, r - 1], rsem_b.at[m, r - 1],
                    seq=2 * z + column,
                )
            )
        kept_z[...] = pick(level)
        return copies

    def stage_cz(m, copies):
        wait(copies)
        kept_z[...] = kept_z[...] + jnp.sum(recv_z[...].astype(f32), axis=0)
        copies = []
        for index, (dx, dy) in enumerate(((1, 1), (1, 0), (0, 1))):
            x = 1 - column if dx else column
            y = 1 - high if dy else high
            send_x[index] = kept_z[x, part_of(y, quarter), :].astype(b16)
            copies.append(
                remote(
                    send_x.at[index], recv_x.at[index], ssem_c.at[m, index], rsem_c.at[m, index],
                    seq=across if dx else me, batch=facing if dy else seat,
                )
            )
        return copies

    def stage_dz(m, copies):
        wait(copies)
        mine = kept_z[column, part_of(high, quarter), :]
        out_w[m, slot] = (mine + jnp.sum(recv_x[...].astype(f32), axis=0)).astype(b16)
        return share(m, out_w.at[m])

    def stage_d(m, copies):
        wait(copies)
        out_w[m, slot] = jnp.sum(recv_c[m].astype(f32), axis=0).astype(b16)
        return share(m, out_w.at[m])

    def rejoin(c):
        return jnp.concatenate(
            [recv2[c, bj, bh] for bh in range(2) for bj in range(mates)], axis=0
        ).T

    wait(own_v)
    vspec[...] = matmul(own_signals(0), table_of(side))
    wait(tap_copies)
    hspec[...] = matmul(both_taps[...].reshape(rows, length), table[...])
    hspec[:, length:] = hspec[:, length:] * sign
    self_v = returned(0, side, vspec[rows_at(side), :], True)
    wait(cross_v)
    vspec[rows_at(other), :] = vspec[rows_at(other), :] + matmul(
        signal(other, other), table_of(other)
    )
    full_v = returned(1, other, vspec[rows_at(other), :], False)
    wait(own_g)
    gspec[...] = matmul(own_signals(1), table_of(side))
    self_g = returned(2, 2 + other, gspec[rows_at(other), :], True)
    r0, s0 = times(gspec[rows_at(other), :], vspec[rows_at(other), :], True)
    r1, s1 = times(gspec[rows_at(side), :], vspec[rows_at(side), :], True)
    fspec[:, :length] = (r0 + r1).astype(b16)
    fspec[:, length:] = ((s0 - s1) * sign).astype(b16)
    acc_f[...] = (matmul_t(fspec[...], table[...]) * (scale / length)).reshape(2, own, length)
    send_af[...] = acc_f[:, part_of(1 - low, 2 * quarter), :].astype(b16)
    af = remote(send_af, recv_af, ssem_a.at[3], rsem_a.at[3], batch=2 * high + 1 - low)
    wait(cross_g)
    whole = gspec[rows_at(side), :] + matmul(signal(2 + side, other), table_of(other))
    full_g = returned(3, 2 + side, whole, False)
    wait(self_v)
    wait(full_v)
    conv = jnp.concatenate([rejoin(0), rejoin(1)], axis=0).astype(f32)
    grad_query = (gates[...].astype(f32) * conv).astype(b16)
    weight(0, matmul(strands_t[...], grad_query))
    a0 = stage_a(0)
    gated = (query[...].astype(f32) * conv).astype(b16)
    weight(1, matmul(gated.T, ups[...]))
    a1 = stage_a(1)
    b0 = stage_b(0, a0)
    b1 = stage_bz(1, a1)
    af.wait()
    kept_f[...] = acc_f[:, part_of(low, 2 * quarter), :] + recv_af[...].astype(f32)
    send_bf[...] = kept_f[:, part_of(1 - high, quarter), :].astype(b16)
    bf = remote(send_bf, recv_bf, ssem_b.at[3, 0], rsem_b.at[3, 0], batch=facing)
    wait(self_g)
    wait(full_g)
    value_0, value_1 = rejoin(2), rejoin(3)
    grad_value = jnp.concatenate([value_0, value_1], axis=0)
    weight(2, matmul(strands_t[...], grad_value))
    a2 = stage_a(2)
    total = strands[...].astype(f32) + matmul(gated, wo[...])
    block_out[:, :half] = total[:here].astype(b16)
    last = total[here:].astype(b16)
    b2 = stage_b(2, a2)
    block_out[:, half:] = matmul(last, flip).astype(b16)
    c0 = stage_c(0, b0)
    c1 = stage_cz(1, b1)
    bf.wait()
    last_f[...] = kept_f[:, part_of(high, quarter), :] + recv_bf[...].astype(f32)
    send_cf[...] = last_f[other].astype(b16)
    cf = remote(send_cf, recv_cf, ssem_c.at[3, 0], rsem_c.at[3, 0], seq=partner)
    total = ups[...].astype(f32) + matmul_t(grad_query, wq[...]) + matmul_t(grad_value, wv[...])
    grad_out[:, :half] = total[:here].astype(b16)
    grad_out[:, half:] = matmul(total[here:].astype(b16), flip).astype(b16)
    d0 = stage_d(0, c0)
    c2 = stage_c(2, b2)
    d1 = stage_dz(1, c1)
    cf.wait()
    out_f[slot] = (last_f[side] + recv_cf[...].astype(f32)).astype(b16)
    df = share(3, out_f)
    wait(d0)
    d2 = stage_d(2, c2)
    wait(d1)
    wait(df)
    wait(d2)


def emit(
    block, grad_tok, weights, filters,
    block_out, grad_out, out_q, out_v, out_o, out_f,
    wide_w, wide_f, sem,
):
    copies = []

    def leave(src, dst):
        copy = pltpu.make_async_copy(src, dst, sem.at[len(copies)])
        copy.start()
        copies.append(copy)

    leave(block, block_out)
    leave(grad_tok, grad_out)
    wide_f[...] = filters[...].reshape(wide_f.shape).astype(wide_f.dtype)
    leave(wide_f, out_f)
    for m, dst in enumerate((out_q, out_o, out_v)):
        wide_w[m] = weights[m].reshape(dst.shape).astype(wide_w.dtype)
        leave(wide_w.at[m], dst)
    for copy in copies:
        copy.wait()


def short_body(tokens, w_query, w_value, w_out, long_filter, cotangent):
    f32, b16 = jnp.float32, jnp.bfloat16
    half = w_query.shape[0]
    peers = lax.axis_size("seq")
    here = tokens.shape[1]
    length = here * peers
    own = half // peers
    scale = (2.0 * lax.axis_size("batch") * length) ** (-0.5)
    coarse, fine = angle_parts(length)
    dma = pltpu.SemaphoreType.DMA
    batches = lax.axis_size("batch")
    quarter = own // batches
    mates = levels = peers // 2
    vmem = pltpu.VMEM
    arguments = (tokens[0], w_query, w_value, w_out, long_filter, cotangent[0], coarse, fine)
    block, grad_tok, weights, filters = pl.pallas_call(
        functools.partial(fused, scale),
        out_shape=(
            vmem((here, 2 * half), b16),
            vmem((here, 2 * half), b16),
            vmem((3, batches, quarter, half), b16),
            vmem((batches, quarter, length), b16),
        ),
        in_specs=[pl.BlockSpec(memory_space=pltpu.HBM)] * 8,
        out_specs=(pl.BlockSpec(memory_space=pltpu.VMEM),) * 4,
        scratch_shapes=[
            *(vmem(a.shape, a.dtype) for a in arguments),
            dma((8,)),
            vmem((length, 2 * length), b16),
            vmem((2 * here, half), b16),
            vmem((2 * here, half), b16),
            vmem((half, 2 * here), b16),
            vmem((2 * here, half), b16),
            vmem((2 * here, half), b16),
            vmem((4, mates, 2, own, here), b16),
            vmem((4, peers, 2, own, here), b16),
            vmem((4, mates, 2, own, here), b16),
            vmem((4, mates, 2, own, here), b16),
            vmem((2, batches, quarter, length), b16),
            vmem((4 * own, 2 * length), f32),
            vmem((4 * own, 2 * length), f32),
            vmem((2 * own, 2 * length), f32),
            vmem((4, 2 * own, 2 * length), b16),
            vmem((2 * own, 2 * length), b16),
            dma((2, peers)),
            dma((2, peers)),
            dma((2,)),
            dma((4, mates)),
            dma((4, mates)),
            dma((4,)),
            dma((batches,)),
            dma((batches,)),
            vmem((3, levels, 2, own, half), f32),
            vmem((3, levels, quarter, half), f32),
            vmem((3, levels, 2, 2 * quarter, half), b16),
            vmem((3, levels, 2, 2 * quarter, half), b16),
            vmem((3, 3, levels, quarter, half), b16),
            vmem((3, 3, levels, quarter, half), b16),
            vmem((3, levels, quarter, half), b16),
            vmem((3, levels, quarter, half), b16),
            vmem((2, 2 * quarter, half), f32),
            vmem((3, 2, 2 * quarter, half), b16),
            vmem((3, 2, 2 * quarter, half), b16),
            vmem((3, quarter, half), b16),
            vmem((3, quarter, half), b16),
            vmem((2, own, length), f32),
            vmem((2, 2 * quarter, length), f32),
            vmem((2, quarter, length), f32),
            vmem((2, 2 * quarter, length), b16),
            vmem((2, 2 * quarter, length), b16),
            vmem((2, quarter, length), b16),
            vmem((2, quarter, length), b16),
            vmem((quarter, length), b16),
            vmem((quarter, length), b16),
            dma((4,)),
            dma((4,)),
            dma((4, 3)),
            dma((4, 3)),
            dma((4, levels)),
            dma((4, levels)),
            dma((4, batches)),
            dma((4, batches)),
        ],
        compiler_params=pltpu.CompilerParams(
            collective_id=0, has_side_effects=True, vmem_limit_bytes=65900000
        ),
    )(*arguments)
    block, grad_tok, *sums = pl.pallas_call(
        emit,
        out_shape=(
            jax.ShapeDtypeStruct((here, 2 * half), b16),
            jax.ShapeDtypeStruct((here, 2 * half), b16),
            jax.ShapeDtypeStruct((own, half), f32),
            jax.ShapeDtypeStruct((own, half), f32),
            jax.ShapeDtypeStruct((own, half), f32),
            jax.ShapeDtypeStruct((own, length), f32),
        ),
        in_specs=[pl.BlockSpec(memory_space=pltpu.VMEM)] * 4,
        out_specs=(pl.BlockSpec(memory_space=pltpu.HBM),) * 6,
        scratch_shapes=[vmem((3, own, half), f32), vmem((own, length), f32), dma((6,))],
        compiler_params=pltpu.CompilerParams(vmem_limit_bytes=8000000),
    )(block, grad_tok, weights, filters)
    return (block[None], grad_tok[None], *sums)


def fits(tokens, half):
    peers, batches = lax.axis_size("seq"), lax.axis_size("batch")
    small = (tokens.shape[1] * peers) ** 2 * 4 <= 8 << 20
    square = peers == 8 and batches == 4 and tokens.shape[1] % 128 == 0
    return small and square and half % (16 * batches * peers) == 0


def choose(tokens, *rest):
    short = fits(tokens, rest[0].shape[0])
    return (short_body if short else body)(tokens, *rest)


def solution(mesh):
    in_specs = (P("batch", "seq", None), P(), P(), P(), P("seq", None), P("batch", "seq", None))
    out_specs = (
        P("batch", "seq", None),
        P("batch", "seq", None),
        P("seq", None),
        P("seq", None),
        P("seq", None),
        P("seq", None),
    )
    return jax.shard_map(choose, mesh=mesh, in_specs=in_specs, out_specs=out_specs, check_vma=False)
```

```python
import functools
import math

import jax
import jax.numpy as jnp
import numpy as np
from jax import lax
from jax.experimental import pallas as pl
from jax.experimental.pallas import tpu as pltpu
from jax.sharding import PartitionSpec as P

precise = lax.Precision.HIGH


def swapped(x, axis, stride):
    return lax.ppermute(x, axis, [(i, i ^ 1 << stride) for i in range(lax.axis_size(axis))])


def angle_tables(count_rows, count_cols, period):
    left = lax.broadcasted_iota(jnp.int32, (count_rows, count_cols), 0)
    right = lax.broadcasted_iota(jnp.int32, (count_rows, count_cols), 1)
    turns = left * right % period
    angle = turns.astype(jnp.float32) * (2.0 * math.pi / period)
    return (jnp.cos(angle), jnp.sin(angle))


def rotation(cosines, sines, direction):
    upper = jnp.stack([cosines, direction * sines])
    lower_row = jnp.stack([-direction * sines, cosines])
    return jnp.stack([upper, lower_row])


def split_sizes(length):
    period = 2 * length
    first = 1 << (period.bit_length() - 1 + 1) // 2
    return (first, period // first)


def make_tables(first, second):
    cos_first, sin_first = angle_tables(first, first, first)
    cos_twist, sin_twist = angle_tables(first, second, first * second)
    cos_second, sin_second = angle_tables(second, second, second)
    forward_first = rotation(cos_first, sin_first, 1.0)
    inverse_first = rotation(cos_first, sin_first, -1.0)
    forward_second = rotation(cos_second, sin_second, 1.0)
    inverse_second = rotation(cos_second, sin_second, -1.0)
    return (forward_first, inverse_first, forward_second, inverse_second, cos_twist, sin_twist)


def forward_spectrum(signal, tables, first, second):
    forward_first, inverse_first, forward_second, inverse_second, cos_twist, sin_twist = tables
    lower = first // 2
    folded = signal.reshape(2, signal.shape[1], lower, second)
    section = jnp.einsum("brnm,abnk->arkm", folded, forward_first[:, :, :lower], precision=precise)
    turned = jnp.stack(
        [
            section[0] * cos_twist + section[1] * sin_twist,
            section[1] * cos_twist - section[0] * sin_twist,
        ]
    )
    return jnp.einsum("brkm,abmj->arkj", turned, forward_second, precision=precise)


def inverse_spectrum(spectrum, tables, first, second, both):
    forward_first, inverse_first, forward_second, inverse_second, cos_twist, sin_twist = tables
    lower = first // 2
    rows = spectrum.shape[1]
    inner = jnp.einsum("brkj,abjm->arkm", spectrum, inverse_second, precision=precise)
    turned = jnp.stack(
        [inner[0] * cos_twist - inner[1] * sin_twist, inner[1] * cos_twist + inner[0] * sin_twist]
    )
    if both:
        signal = jnp.einsum(
            "brkm,abkn->arnm", turned, inverse_first[:, :, :, :lower], precision=precise
        )
        return (signal / (first * second)).reshape(2, rows, lower * second)
    signal = jnp.einsum("brkm,bkn->rnm", turned, inverse_first[0][:, :, :lower], precision=precise)
    return (signal / (first * second)).reshape(rows, lower * second)


def complex_product(left, right):
    return jnp.stack(
        [left[0] * right[0] - left[1] * right[1], left[0] * right[1] + left[1] * right[0]]
    )


def conjugate_product(left, right):
    return jnp.stack(
        [left[0] * right[0] + left[1] * right[1], left[0] * right[1] - left[1] * right[0]]
    )


def mirror(array, seq_dim):
    moved = array
    for bit_index in range(lax.axis_size("seq").bit_length() - 1):
        moved = swapped(moved, "seq", bit_index)
    return jnp.flip(moved, axis=seq_dim)


def to_channels(stacked):
    return lax.all_to_all(stacked, "seq", split_axis=1, concat_axis=2, tiled=True)


def to_tokens(stacked):
    return lax.all_to_all(stacked, "seq", split_axis=2, concat_axis=1, tiled=True)


def body(tokens, w_query, w_value, w_out, long_filter, cotangent):
    floats = jnp.float32
    halves = jnp.bfloat16
    half = w_query.shape[0]
    seq_count = lax.axis_size("seq")
    batch_count = lax.axis_size("batch")
    length = tokens.shape[1] * seq_count
    first, second = split_sizes(length)
    tables = make_tables(first, second)
    scale = (2.0 * batch_count * length) ** (-0.5)
    source = tokens[0]
    front = source[:, :half]
    back = source[:, half:]
    back_strand = mirror(back, 0)[:, ::-1]
    strands = jnp.stack([front, back_strand])
    query = jnp.einsum("stk,kh->sht", strands, w_query, preferred_element_type=floats).astype(
        halves
    )
    value = jnp.einsum("stk,kh->sht", strands, w_value, preferred_element_type=floats).astype(
        halves
    )
    value_sig = to_channels(value).astype(floats)
    value_spec = forward_spectrum(value_sig, tables, first, second)
    taps_spec = forward_spectrum(
        jnp.stack([long_filter, jnp.zeros_like(long_filter)]), tables, first, second
    )
    conv_sig = inverse_spectrum(complex_product(value_spec, taps_spec), tables, first, second, True)
    conv_tok = to_tokens(conv_sig.astype(halves))
    gated = (query.astype(floats) * conv_tok.astype(floats)).astype(halves)
    gated_back = mirror(gated[1], 1)
    out_front = jnp.einsum("ht,hk->tk", gated[0], w_out, preferred_element_type=floats)
    out_back = jnp.einsum("ht,hk->tk", gated_back, w_out, preferred_element_type=floats)
    block_out = jnp.concatenate(
        [front.astype(floats) + out_front, back.astype(floats) + out_back[:, ::-1]], axis=1
    ).astype(halves)[None]
    upstream = cotangent[0]
    up_front = upstream[:, :half]
    up_back = upstream[:, half:]
    grad_back = mirror(up_back, 0)[:, ::-1]
    grad_strands = jnp.stack([up_front, grad_back])
    grad_gated = jnp.einsum(
        "stk,hk->sht", grad_strands, w_out, preferred_element_type=floats
    ).astype(halves)
    grad_query_t = (grad_gated.astype(floats) * conv_tok.astype(floats)).astype(halves)
    grad_conv = (grad_gated.astype(floats) * query.astype(floats)).astype(halves)
    grad_sig = to_channels(grad_conv).astype(floats)
    grad_spec = forward_spectrum(grad_sig, tables, first, second)
    value_grad_sig = inverse_spectrum(
        conjugate_product(taps_spec, grad_spec), tables, first, second, True
    )
    filter_part = (
        inverse_spectrum(conjugate_product(value_spec, grad_spec), tables, first, second, False)
        * scale
    )
    grad_value_t = to_tokens(value_grad_sig.astype(halves))
    front_in = jnp.einsum(
        "ht,kh->tk", grad_query_t[0], w_query, preferred_element_type=floats
    ) + jnp.einsum("ht,kh->tk", grad_value_t[0], w_value, preferred_element_type=floats)
    paired = jnp.stack([grad_query_t[1], grad_value_t[1]])
    paired = mirror(paired, 2)
    back_in = jnp.einsum(
        "ht,kh->tk", paired[0], w_query, preferred_element_type=floats
    ) + jnp.einsum("ht,kh->tk", paired[1], w_value, preferred_element_type=floats)
    grad_tokens = jnp.concatenate(
        [up_front.astype(floats) + front_in, up_back.astype(floats) + back_in[:, ::-1]], axis=1
    ).astype(halves)[None]
    term_query = jnp.einsum("stk,sht->kh", strands, grad_query_t, preferred_element_type=floats)
    term_value = jnp.einsum("stk,sht->kh", strands, grad_value_t, preferred_element_type=floats)
    term_out = jnp.einsum("sht,stk->hk", gated, grad_strands, preferred_element_type=floats)
    share = lax.psum_scatter(
        jnp.concatenate([term_query, term_value, term_out], axis=1) * scale,
        "seq",
        scatter_dimension=0,
        tiled=True,
    )
    share, filter_total = (
        lax.psum(share.astype(jnp.bfloat16), "batch").astype(jnp.float32),
        lax.psum(filter_part.astype(jnp.bfloat16), "batch").astype(jnp.float32),
    )
    return (
        block_out,
        grad_tokens,
        share[:, :half],
        share[:, half : 2 * half],
        share[:, 2 * half :],
        filter_total,
    )

MESH = pl.DeviceIdType.MESH


def angle_parts(length):
    step = 1 << (length.bit_length() - 1) // 2
    angle = np.pi * (np.arange(length) + 0.5)[None] / length
    coarse = np.arange(length // step)[:, None] * step * angle
    fine = np.arange(step)[:, None] * angle
    return (
        np.stack([np.cos(coarse), np.sin(coarse)]).astype(np.float32),
        np.stack([np.cos(fine), np.sin(fine)]).astype(np.float32),
    )


def matmul(left, right):
    return jnp.dot(left, right, preferred_element_type=jnp.float32)


def matmul_t(left, right):
    return lax.dot_general(
        left, right, (((1,), (1,)), ((), ())), preferred_element_type=jnp.float32
    )


def times(x, h, conj):
    size = x.shape[1] // 2
    xr, xs, hr, hs = x[:, :size], x[:, size:], h[:, :size], h[:, size:]
    if conj:
        return xr * hr + xs * hs, xs * hr - xr * hs
    return xr * hr - xs * hs, xr * hs + xs * hr


def fused(
    scale,
    tok_in, wq_in, wv_in, wo_in, taps_in, cot_in, coarse_in, fine_in,
    block_out, grad_out, out_w, out_f,
    tok, wq, wv, wo, taps, cot, coarse, fine, lsem,
    table, strands, ups, strands_t, query, gates, send1, recv1, send2, recv2,
    both_taps, vspec, gspec, hspec, yspec, fspec,
    ssem1, rsem1, lsem1, ssem2, rsem2, lsem2, ssem_t, rsem_t,
    acc, kept, send_a, recv_a, send_b, recv_b, send_c, recv_c,
    kept_z, send_z, recv_z, send_x, recv_x,
    acc_f, kept_f, last_f, send_af, recv_af, send_bf, recv_bf, send_cf, recv_cf,
    ssem_a, rsem_a, ssem_b, rsem_b, ssem_c, rsem_c, ssem_d, rsem_d,
):
    peers, batches = lax.axis_size("seq"), lax.axis_size("batch")
    me, seat = lax.axis_index("seq"), lax.axis_index("batch")
    here, half = tok.shape[0], wq.shape[0]
    f32, b16 = jnp.float32, jnp.bfloat16
    own = half // peers
    length = here * peers
    quarter = own // batches
    mates = peers // 2
    wide = mates * here
    rows = 2 * own
    side, seat_in_side = me // mates, lax.rem(me, mates)
    other = 1 - side
    sign = (2 * side - 1).astype(f32)
    column, level = lax.rem(me, 2), me // 2
    levels = peers // 2
    low, high = lax.rem(seat, 2), seat // 2
    slot = 2 * low + high

    barrier = pltpu.get_barrier_semaphore()
    across = me + 1 - 2 * column
    facing = seat + 2 - 4 * high
    for r in range(1, peers):
        pl.semaphore_signal(
            barrier, inc=1, device_id={"seq": lax.rem(me + r, peers)}, device_id_type=MESH
        )
    for r in range(1, batches):
        pl.semaphore_signal(
            barrier, inc=1, device_id={"batch": lax.rem(seat + r, batches)}, device_id_type=MESH
        )
    pl.semaphore_signal(
        barrier, inc=1, device_id={"seq": across, "batch": facing}, device_id_type=MESH
    )
    loads = {}
    pairs = (
        ("tok", tok_in, tok), ("wv", wv_in, wv), ("taps", taps_in, taps), ("cot", cot_in, cot),
        ("wo", wo_in, wo), ("wq", wq_in, wq), ("coarse", coarse_in, coarse), ("fine", fine_in, fine),
    )
    for index, (name, src, dst) in enumerate(pairs):
        loads[name] = pltpu.make_async_copy(src, dst, lsem.at[index])
        loads[name].start()

    def remote(src, dst, ssem, rsem, **device):
        copy = pltpu.make_async_remote_copy(
            src_ref=src, dst_ref=dst, send_sem=ssem, recv_sem=rsem,
            device_id=device, device_id_type=MESH,
        )
        copy.start()
        return copy

    def local(src, dst, sem):
        copy = pltpu.make_async_copy(src, dst, sem)
        copy.start()
        return copy

    def wait(copies):
        for c in copies:
            c.wait()

    flip = (
        lax.broadcasted_iota(jnp.int32, (half, half), 0)
        + lax.broadcasted_iota(jnp.int32, (half, half), 1)
        == half - 1
    ).astype(f32).astype(b16)

    def stage_rows(index, x):
        turned = x.T
        for bh in range(2):
            for bj in range(mates):
                start = (bh * mates + bj) * own
                send1[index, bj, bh] = turned[start : start + own]

    loads["tok"].wait()
    strands[:here] = tok[:, :half]
    strands[here:] = matmul(tok[:, half:], flip).astype(b16)
    loads["wv"].wait()
    value = matmul(strands[...], wv[...]).astype(b16)
    stage_rows(0, value[:here])
    stage_rows(1, value[here:])
    loads["taps"].wait()
    both_taps[pl.ds(side, 1)] = taps[...].astype(b16).reshape(1, batches, quarter, length)
    pl.semaphore_wait(barrier, peers + batches - 1)

    partner = lax.rem(me + mates, peers)
    tap_copy = remote(
        both_taps.at[side, seat], both_taps.at[side, seat], ssem_t.at[0], rsem_t.at[0], seq=partner
    )

    def out1_cross(d):
        c = 2 * d + (side if d == 0 else other)
        copies = []
        for r in range(mates):
            q = lax.rem(seat_in_side + r, mates)
            copies.append(
                remote(
                    send1.at[c, q], recv1.at[c, me], ssem1.at[d, mates + r], rsem1.at[d, mates + r],
                    seq=other * mates + q,
                )
            )
        return copies

    def out1_own(d):
        pair = pl.ds(2 * d, 2)
        copies = []
        for r in range(1, mates):
            q = lax.rem(seat_in_side + r, mates)
            copies.append(
                remote(
                    send1.at[pair, q], recv1.at[pair, me], ssem1.at[d, r], rsem1.at[d, r],
                    seq=side * mates + q,
                )
            )
        copies.append(local(send1.at[pair, seat_in_side], recv1.at[pair, me], lsem1.at[d]))
        return copies

    def out2(k, c):
        copies = []
        for r in range(1, mates):
            q = lax.rem(seat_in_side + r, mates)
            copies.append(
                remote(
                    send2.at[c, q], recv2.at[c, seat_in_side], ssem2.at[k, r], rsem2.at[k, r],
                    seq=side * mates + q,
                )
            )
        copies.append(local(send2.at[c, seat_in_side], recv2.at[c, seat_in_side], lsem2.at[k]))
        return copies

    own_v = out1_own(0)
    cross_v = out1_cross(0)

    for name in ("cot", "wo", "wq"):
        loads[name].wait()
    ups[:here] = cot[:, :half]
    ups[here:] = matmul(cot[:, half:], flip).astype(b16)
    query[...] = matmul(strands[...], wq[...]).astype(b16)
    gates[...] = matmul_t(ups[...], wo[...]).astype(b16)
    grad_conv = (gates[...].astype(f32) * query[...].astype(f32)).astype(b16)
    stage_rows(2, grad_conv[:here])
    stage_rows(3, grad_conv[here:])
    own_g = out1_own(1)
    cross_g = out1_cross(1)

    for name in ("coarse", "fine"):
        loads[name].wait()
    count, step = coarse.shape[1], fine.shape[1]

    @pl.loop(0, count)
    def _(a):
        ca, sa = coarse[0, pl.ds(a, 1), :], coarse[1, pl.ds(a, 1), :]
        at = pl.ds(pl.multiple_of(a * step, step), step)
        table[at, :length] = (ca * fine[0] - sa * fine[1]).astype(b16)
        table[at, length:] = (sa * fine[0] + ca * fine[1]).astype(b16)

    tap_copy.wait()
    tap_copies = [
        remote(
            both_taps.at[other, seat], both_taps.at[other, seat], ssem_t.at[r], rsem_t.at[r],
            batch=lax.rem(seat + r, batches),
        )
        for r in range(1, batches)
    ]
    strands_t[...] = strands[...].T

    def rows_at(i):
        return pl.ds(pl.multiple_of(i * rows, rows), rows)

    def table_of(which):
        return table[pl.ds(pl.multiple_of(which * wide, wide), wide), :]

    def signal(c, which):
        return jnp.concatenate(
            [recv1[c, which * mates + i].reshape(rows, here) for i in range(mates)], axis=1
        )

    def own_signals(d):
        return jnp.concatenate([signal(2 * d, side), signal(2 * d + 1, side)], axis=0)

    def returned(k, c, spec, conj):
        r, s = times(spec, hspec[...], conj)
        yspec[k, :, :length] = r.astype(b16)
        yspec[k, :, length:] = s.astype(b16)
        back = (matmul_t(yspec[k], table_of(side)) * (1.0 / length)).astype(b16)
        for q in range(mates):
            send2[pl.ds(c, 1), q] = back[:, q * here : (q + 1) * here].reshape(1, 2, own, here)
        return out2(k, c)

    def part_of(bit, size):
        return pl.ds(pl.multiple_of(bit * size, size), size)

    def weight(m, product):
        acc[m] = (product * scale).reshape(levels, 2, own, half)

    def stage_a(m):
        send_a[m] = acc[m, :, :, part_of(1 - low, 2 * quarter), :].astype(b16)
        return remote(
            send_a.at[m], recv_a.at[m], ssem_a.at[m], rsem_a.at[m], batch=2 * high + 1 - low
        )

    def stage_b(m, copy):
        copy.wait()

        def pick(x, y):
            at = pl.ds(pl.multiple_of((2 * low + y) * quarter, quarter), quarter)
            mine = acc[m, :, pl.ds(x, 1), at, :]
            theirs = recv_a[m, :, pl.ds(x, 1), part_of(y, quarter), :].astype(f32)
            return (mine + theirs).reshape(levels, quarter, half)

        copies = []
        for index, (dx, dy) in enumerate(((0, 1), (1, 0), (1, 1))):
            x = 1 - column if dx else column
            y = 1 - high if dy else high
            send_b[m, index] = pick(x, y).astype(b16)
            copies.append(
                remote(
                    send_b.at[m, index], recv_b.at[m, index], ssem_b.at[m, index],
                    rsem_b.at[m, index], seq=across if dx else me, batch=facing if dy else seat,
                )
            )
        kept[m] = pick(column, high)
        return copies

    def stage_c(m, copies):
        wait(copies)
        send_c[m] = (kept[m] + jnp.sum(recv_b[m].astype(f32), axis=0)).astype(b16)
        copies = []
        for r in range(1, levels):
            z = lax.rem(level + r, levels)
            copies.append(
                remote(
                    send_c.at[m, z], recv_c.at[m, level], ssem_c.at[m, r], rsem_c.at[m, r],
                    seq=2 * z + column,
                )
            )
        recv_c[m, level] = send_c[m, level]
        return copies

    def share(m, whole):
        return [
            remote(
                whole.at[slot], whole.at[slot], ssem_d.at[m, r], rsem_d.at[m, r],
                batch=lax.rem(seat + r, batches),
            )
            for r in range(1, batches)
        ]

    def stage_bz(m, copy):
        copy.wait()

        def pick(z):
            mine = acc[m, pl.ds(z, 1), :, part_of(low, 2 * quarter), :]
            return (mine + recv_a[m, pl.ds(z, 1)].astype(f32)).reshape(2, 2 * quarter, half)

        copies = []
        for r in range(1, levels):
            z = lax.rem(level + r, levels)
            send_z[r - 1] = pick(z).astype(b16)
            copies.append(
                remote(
                    send_z.at[r - 1], recv_z.at[r - 1], ssem_b.at[m, r - 1], rsem_b.at[m, r - 1],
                    seq=2 * z + column,
                )
            )
        kept_z[...] = pick(level)
        return copies

    def stage_cz(m, copies):
        wait(copies)
        kept_z[...] = kept_z[...] + jnp.sum(recv_z[...].astype(f32), axis=0)
        copies = []
        for index, (dx, dy) in enumerate(((0, 1), (1, 0), (1, 1))):
            x = 1 - column if dx else column
            y = 1 - high if dy else high
            send_x[index] = kept_z[x, part_of(y, quarter), :].astype(b16)
            copies.append(
                remote(
                    send_x.at[index], recv_x.at[index], ssem_c.at[m, index], rsem_c.at[m, index],
                    seq=across if dx else me, batch=facing if dy else seat,
                )
            )
        return copies

    def stage_dz(m, copies):
        wait(copies)
        mine = kept_z[column, part_of(high, quarter), :]
        out_w[m, slot] = (mine + jnp.sum(recv_x[...].astype(f32), axis=0)).astype(b16)
        return share(m, out_w.at[m])

    def stage_d(m, copies):
        wait(copies)
        out_w[m, slot] = jnp.sum(recv_c[m].astype(f32), axis=0).astype(b16)
        return share(m, out_w.at[m])

    def rejoin(c):
        return jnp.concatenate(
            [recv2[c, bj, bh] for bh in range(2) for bj in range(mates)], axis=0
        ).T

    wait(own_v)
    vspec[...] = matmul(own_signals(0), table_of(side))
    wait(tap_copies)
    hspec[...] = matmul(both_taps[...].reshape(rows, length), table[...])
    hspec[:, length:] = hspec[:, length:] * sign
    self_v = returned(0, side, vspec[rows_at(side), :], True)
    wait(cross_v)
    vspec[rows_at(other), :] = vspec[rows_at(other), :] + matmul(
        signal(other, other), table_of(other)
    )
    full_v = returned(1, other, vspec[rows_at(other), :], False)
    wait(own_g)
    gspec[...] = matmul(own_signals(1), table_of(side))
    self_g = returned(2, 2 + other, gspec[rows_at(other), :], True)
    r0, s0 = times(gspec[rows_at(other), :], vspec[rows_at(other), :], True)
    r1, s1 = times(gspec[rows_at(side), :], vspec[rows_at(side), :], True)
    fspec[:, :length] = (r0 + r1).astype(b16)
    fspec[:, length:] = ((s0 - s1) * sign).astype(b16)
    acc_f[...] = (matmul_t(fspec[...], table[...]) * (scale / length)).reshape(2, own, length)
    send_af[...] = acc_f[:, part_of(1 - low, 2 * quarter), :].astype(b16)
    af = remote(send_af, recv_af, ssem_a.at[3], rsem_a.at[3], batch=2 * high + 1 - low)
    wait(cross_g)
    whole = gspec[rows_at(side), :] + matmul(signal(2 + side, other), table_of(other))
    full_g = returned(3, 2 + side, whole, False)
    wait(self_v)
    wait(full_v)
    conv = jnp.concatenate([rejoin(0), rejoin(1)], axis=0).astype(f32)
    grad_query = (gates[...].astype(f32) * conv).astype(b16)
    weight(0, matmul(strands_t[...], grad_query))
    a0 = stage_a(0)
    gated = (query[...].astype(f32) * conv).astype(b16)
    weight(1, matmul(gated.T, ups[...]))
    a1 = stage_a(1)
    b0 = stage_b(0, a0)
    b1 = stage_bz(1, a1)
    af.wait()
    kept_f[...] = acc_f[:, part_of(low, 2 * quarter), :] + recv_af[...].astype(f32)
    send_bf[...] = kept_f[:, part_of(1 - high, quarter), :].astype(b16)
    bf = remote(send_bf, recv_bf, ssem_b.at[3, 0], rsem_b.at[3, 0], batch=facing)
    wait(self_g)
    wait(full_g)
    value_0, value_1 = rejoin(2), rejoin(3)
    grad_value = jnp.concatenate([value_0, value_1], axis=0)
    weight(2, matmul(strands_t[...], grad_value))
    a2 = stage_a(2)
    total = strands[...].astype(f32) + matmul(gated, wo[...])
    block_out[:, :half] = total[:here].astype(b16)
    last = total[here:].astype(b16)
    b2 = stage_b(2, a2)
    block_out[:, half:] = matmul(last, flip).astype(b16)
    c0 = stage_c(0, b0)
    c1 = stage_cz(1, b1)
    bf.wait()
    last_f[...] = kept_f[:, part_of(high, quarter), :] + recv_bf[...].astype(f32)
    send_cf[...] = last_f[other].astype(b16)
    cf = remote(send_cf, recv_cf, ssem_c.at[3, 0], rsem_c.at[3, 0], seq=partner)
    total = ups[...].astype(f32) + matmul_t(grad_query, wq[...]) + matmul_t(grad_value, wv[...])
    grad_out[:, :half] = total[:here].astype(b16)
    grad_out[:, half:] = matmul(total[here:].astype(b16), flip).astype(b16)
    d0 = stage_d(0, c0)
    c2 = stage_c(2, b2)
    d1 = stage_dz(1, c1)
    cf.wait()
    out_f[slot] = (last_f[side] + recv_cf[...].astype(f32)).astype(b16)
    df = share(3, out_f)
    wait(d0)
    d2 = stage_d(2, c2)
    wait(d1)
    wait(df)
    wait(d2)


def emit(
    block, grad_tok, weights, filters,
    block_out, grad_out, out_q, out_v, out_o, out_f,
    wide_w, wide_f, sem,
):
    copies = []

    def leave(src, dst):
        copy = pltpu.make_async_copy(src, dst, sem.at[len(copies)])
        copy.start()
        copies.append(copy)

    leave(block, block_out)
    leave(grad_tok, grad_out)
    wide_f[...] = filters[...].reshape(wide_f.shape).astype(wide_f.dtype)
    leave(wide_f, out_f)
    for m, dst in enumerate((out_q, out_o, out_v)):
        wide_w[m] = weights[m].reshape(dst.shape).astype(wide_w.dtype)
        leave(wide_w.at[m], dst)
    for copy in copies:
        copy.wait()


def short_body(tokens, w_query, w_value, w_out, long_filter, cotangent):
    f32, b16 = jnp.float32, jnp.bfloat16
    half = w_query.shape[0]
    peers = lax.axis_size("seq")
    here = tokens.shape[1]
    length = here * peers
    own = half // peers
    scale = (2.0 * lax.axis_size("batch") * length) ** (-0.5)
    coarse, fine = angle_parts(length)
    dma = pltpu.SemaphoreType.DMA
    batches = lax.axis_size("batch")
    quarter = own // batches
    mates = levels = peers // 2
    vmem = pltpu.VMEM
    arguments = (tokens[0], w_query, w_value, w_out, long_filter, cotangent[0], coarse, fine)
    block, grad_tok, weights, filters = pl.pallas_call(
        functools.partial(fused, scale),
        out_shape=(
            vmem((here, 2 * half), b16),
            vmem((here, 2 * half), b16),
            vmem((3, batches, quarter, half), b16),
            vmem((batches, quarter, length), b16),
        ),
        in_specs=[pl.BlockSpec(memory_space=pltpu.HBM)] * 8,
        out_specs=(pl.BlockSpec(memory_space=pltpu.VMEM),) * 4,
        scratch_shapes=[
            *(vmem(a.shape, a.dtype) for a in arguments),
            dma((8,)),
            vmem((length, 2 * length), b16),
            vmem((2 * here, half), b16),
            vmem((2 * here, half), b16),
            vmem((half, 2 * here), b16),
            vmem((2 * here, half), b16),
            vmem((2 * here, half), b16),
            vmem((4, mates, 2, own, here), b16),
            vmem((4, peers, 2, own, here), b16),
            vmem((4, mates, 2, own, here), b16),
            vmem((4, mates, 2, own, here), b16),
            vmem((2, batches, quarter, length), b16),
            vmem((4 * own, 2 * length), f32),
            vmem((4 * own, 2 * length), f32),
            vmem((2 * own, 2 * length), f32),
            vmem((4, 2 * own, 2 * length), b16),
            vmem((2 * own, 2 * length), b16),
            dma((2, peers)),
            dma((2, peers)),
            dma((2,)),
            dma((4, mates)),
            dma((4, mates)),
            dma((4,)),
            dma((batches,)),
            dma((batches,)),
            vmem((3, levels, 2, own, half), f32),
            vmem((3, levels, quarter, half), f32),
            vmem((3, levels, 2, 2 * quarter, half), b16),
            vmem((3, levels, 2, 2 * quarter, half), b16),
            vmem((3, 3, levels, quarter, half), b16),
            vmem((3, 3, levels, quarter, half), b16),
            vmem((3, levels, quarter, half), b16),
            vmem((3, levels, quarter, half), b16),
            vmem((2, 2 * quarter, half), f32),
            vmem((3, 2, 2 * quarter, half), b16),
            vmem((3, 2, 2 * quarter, half), b16),
            vmem((3, quarter, half), b16),
            vmem((3, quarter, half), b16),
            vmem((2, own, length), f32),
            vmem((2, 2 * quarter, length), f32),
            vmem((2, quarter, length), f32),
            vmem((2, 2 * quarter, length), b16),
            vmem((2, 2 * quarter, length), b16),
            vmem((2, quarter, length), b16),
            vmem((2, quarter, length), b16),
            vmem((quarter, length), b16),
            vmem((quarter, length), b16),
            dma((4,)),
            dma((4,)),
            dma((4, 3)),
            dma((4, 3)),
            dma((4, levels)),
            dma((4, levels)),
            dma((4, batches)),
            dma((4, batches)),
        ],
        compiler_params=pltpu.CompilerParams(
            collective_id=0, has_side_effects=True, vmem_limit_bytes=65900000
        ),
    )(*arguments)
    block, grad_tok, *sums = pl.pallas_call(
        emit,
        out_shape=(
            jax.ShapeDtypeStruct((here, 2 * half), b16),
            jax.ShapeDtypeStruct((here, 2 * half), b16),
            jax.ShapeDtypeStruct((own, half), f32),
            jax.ShapeDtypeStruct((own, half), f32),
            jax.ShapeDtypeStruct((own, half), f32),
            jax.ShapeDtypeStruct((own, length), f32),
        ),
        in_specs=[pl.BlockSpec(memory_space=pltpu.VMEM)] * 4,
        out_specs=(pl.BlockSpec(memory_space=pltpu.HBM),) * 6,
        scratch_shapes=[vmem((3, own, half), f32), vmem((own, length), f32), dma((6,))],
        compiler_params=pltpu.CompilerParams(vmem_limit_bytes=8000000),
    )(block, grad_tok, weights, filters)
    return (block[None], grad_tok[None], *sums)


def fits(tokens, half):
    peers, batches = lax.axis_size("seq"), lax.axis_size("batch")
    small = (tokens.shape[1] * peers) ** 2 * 4 <= 8 << 20
    square = peers == 8 and batches == 4 and tokens.shape[1] % 128 == 0
    return small and square and half % (16 * batches * peers) == 0


def choose(tokens, *rest):
    short = fits(tokens, rest[0].shape[0])
    return (short_body if short else body)(tokens, *rest)


def solution(mesh):
    in_specs = (P("batch", "seq", None), P(), P(), P(), P("seq", None), P("batch", "seq", None))
    out_specs = (
        P("batch", "seq", None),
        P("batch", "seq", None),
        P("seq", None),
        P("seq", None),
        P("seq", None),
        P("seq", None),
    )
    return jax.shard_map(choose, mesh=mesh, in_specs=in_specs, out_specs=out_specs, check_vma=False)
```
